512 devices in a mesh: dict: 16 (over z, core), scan: 32 (over x, y).
Axes of the slice: x: 4, y: 8, z: 8, core: 2. Of those that a mesh axis runs over, the one named last changes fastest.
Arguments:
- patterns: float32 [512, 256, 3600], P('scan', 'dict'), may hold values from -63 to 63
- background: float32 [3600], replicated, may hold values from -6 to 6
- templates: bfloat16 [2048, 3600], P('dict'), may hold values from -19.5 to 19.5
- grain_id: int32 [512, 256], P('scan', 'dict'), may hold values from 0 to 127
- keep_mask: int32 [512, 256], P('scan', 'dict'), may hold values 0 or 1
- grain_row: int32 [128], replicated, may hold values from 0 to 127, each once
Outputs:
- max_score: float32 [512, 256], P('scan', 'dict')
- grain_patterns: float32 [128, 3600], P('scan')
The draws below stay inside these ranges and needn't reach their ends.
Inputs may be any that keep to these rules, and one draw needn't show every extreme that they name: grain_row holds each of 0 to 127 once.
All inputs are finite; a program needn't handle non-finite values. No bound on the sum of `keep_mask` on one device may be relied on, other than what follows from the above.
Results may differ from the reference program's by a relative error of at most 0.0045.
Values may be sent and summed in bfloat16 or wider, within the bound.
No kernel may reach another device: no remote copies, remote signals or barrier semaphores. Data moves between devices by JAX's collectives and lax.ppermute only.
A program may use at most 128 MiB of HBM per device.

```python
import math
import jax
import jax.numpy as jnp
import numpy as np
from jax import lax

PIX = 3600
SCAN_ROWS = 512
SCAN_COLS = 256
TEMPLATES = 2048
GRAINS = 128


def draw_patterns(key, part):
    noise_key = jax.random.fold_in(key, 11)
    scale_key = jax.random.fold_in(key, 12)
    shift_key = jax.random.fold_in(key, 13)
    full_shape = (SCAN_ROWS, SCAN_COLS, PIX)
    point_shape = (SCAN_ROWS, SCAN_COLS, 1)
    values_raw = jnp.clip(jax.random.normal(noise_key, full_shape, jnp.float32), -6.0, 6.0)
    spread = jnp.exp(jax.random.uniform(scale_key, point_shape, jnp.float32, 0.0, math.log(10.0)))
    offset = jax.random.uniform(shift_key, point_shape, jnp.float32, -3.0, 3.0)
    return values_raw * spread + offset


def draw_templates(key, part):
    noise_key = jax.random.fold_in(key, 21)
    scale_key = jax.random.fold_in(key, 22)
    shift_key = jax.random.fold_in(key, 23)
    full_shape = (TEMPLATES, PIX)
    template_shape = (TEMPLATES, 1)
    values_raw = jnp.clip(jax.random.normal(noise_key, full_shape, jnp.float32), -6.0, 6.0)
    spread = jnp.exp(jax.random.uniform(scale_key, template_shape, jnp.float32, math.log(0.3), math.log(3.0)))
    offset = jax.random.uniform(shift_key, template_shape, jnp.float32, -1.5, 1.5)
    return (values_raw * spread + offset).astype(jnp.bfloat16)


def with_ends(drawn, rng, smallest, largest):
    shape = drawn.shape
    place = [jax.random.randint(jax.random.fold_in(rng, axis), (), 0, shape[axis]) for axis in range(len(shape))]
    drawn = drawn.at[tuple(place)].set(smallest)
    longest = shape.index(max(shape))
    place[longest] = (place[longest] + 1) % shape[longest]
    return drawn.at[tuple(place)].set(largest)


def rank_bounds(amount, lean):
    loads = [(1 << 20) // math.isqrt(rank ** lean) + 1 for rank in range(1, amount + 1)]
    scale = 1 + sum(loads) // (1 << 30)
    return np.cumsum(np.array([max(1, weight // scale) for weight in loads]))


def skewed_ids(stream_key, shape, amount, skew):
    table = rank_bounds(amount, skew)
    ticket = jax.random.randint(jax.random.fold_in(stream_key, 1), shape, 0, int(table[amount - 1]))
    standing = jnp.searchsorted(jnp.asarray(table, jnp.int32), ticket, side="right")
    return jax.random.permutation(jax.random.fold_in(stream_key, 2), amount)[standing].astype(jnp.int32)


def scatter_about(rng, dims, deviation, limit, held_as=jnp.bfloat16):
    entries = jax.random.normal(rng, dims, jnp.float32) * deviation
    return jnp.minimum(jnp.maximum(entries, -limit), limit).astype(held_as)


def setup_inputs(seed: int = 0) -> dict:
    key_of = jax.random.split(jax.random.key(seed), 7)
    return {
        "patterns": draw_patterns(jax.random.fold_in(key_of[6], 71), 0),
        "background": scatter_about(key_of[1], (PIX,), 1.0, 6.0, jnp.float32),
        "templates": draw_templates(jax.random.fold_in(key_of[6], 71), 0),
        "grain_id": with_ends(skewed_ids(key_of[3], (SCAN_ROWS, SCAN_COLS), GRAINS, 2), jax.random.fold_in(key_of[3], 3), 0, GRAINS - 1).astype(jnp.int32),
        "keep_mask": with_ends((jax.random.randint(key_of[4], (SCAN_ROWS, SCAN_COLS), 0, 4) < 3).astype(jnp.int32), jax.random.fold_in(key_of[4], 1), 0, 1),
        "grain_row": jax.random.permutation(key_of[5], GRAINS).astype(jnp.int32),
    }


def unit_rows(values):
    mean_square = lax.optimization_barrier(jnp.mean(values * values, axis=-1, keepdims=True))
    return values * lax.rsqrt(mean_square + 1e-05)

def filter_points(measured, background):
    centered = measured - background
    centered = centered - lax.optimization_barrier(jnp.mean(centered, axis=-1, keepdims=True))
    return unit_rows(centered).astype(jnp.bfloat16)

def reference(patterns, background, templates, grain_id, keep_mask, grain_row):

    def filter_one(measured_row):
        return filter_points(measured_row, background)
    filtered = lax.map(filter_one, patterns)
    padded = jnp.pad(filtered, ((1, 1), (1, 1), (0, 0)))
    centered_panel = templates.astype(jnp.float32)
    centered_panel = centered_panel - lax.optimization_barrier(jnp.mean(centered_panel, axis=-1, keepdims=True))
    unit_panel = unit_rows(centered_panel).astype(jnp.bfloat16)
    grain_index = jnp.arange(GRAINS, dtype=jnp.int32)
    point_rows = lax.optimization_barrier(jnp.sum(jnp.where(grain_id[:, :, None] == grain_index, grain_row, 0), axis=2)).astype(jnp.int32)
    root_inverse = 1.0 / math.sqrt(PIX)

    def one_row(totals, row_number):
        row_block = lax.dynamic_slice_in_dim(padded, row_number, 3, 0)
        neighbour = jnp.zeros((SCAN_COLS, PIX), jnp.float32)
        for row_shift in range(3):
            for col_shift in range(3):
                neighbour = neighbour + row_block[row_shift, col_shift:col_shift + SCAN_COLS].astype(jnp.float32)
        indexed = unit_rows(neighbour).astype(jnp.bfloat16)
        scores = lax.dot_general(indexed, unit_panel, (((1,), (1,)), ((), ())), preferred_element_type=jnp.float32)
        best_row = lax.optimization_barrier(jnp.max(scores, axis=1)) * root_inverse
        row_of_points = lax.dynamic_index_in_dim(point_rows, row_number, 0, keepdims=False)
        keep_row = lax.dynamic_index_in_dim(keep_mask, row_number, 0, keepdims=False)
        selector = ((row_of_points[:, None] == grain_index[None, :]) & (keep_row[:, None] == 1)).astype(jnp.bfloat16)
        totals = totals + lax.dot_general(selector, indexed, (((0,), (0,)), ((), ())), preferred_element_type=jnp.float32)
        return (totals, best_row)
    totals, max_score = lax.scan(one_row, jnp.zeros((GRAINS, PIX), jnp.float32), jnp.arange(SCAN_ROWS, dtype=jnp.int32))
    return (max_score, unit_rows(totals))
```

```python
import math

import jax
import jax.numpy as jnp
from jax import lax
from jax.sharding import PartitionSpec as P


def with_halo(block, sides, width):
    for axis, dim in sides:
        count = lax.axis_size(axis)
        forward = [(i, i + 1) for i in range(count - 1)]
        backward = [(target, source) for source, target in forward]
        low = lax.ppermute(
            lax.slice_in_dim(block, block.shape[dim] - width, None, axis=dim), axis, forward
        )
        high = lax.ppermute(lax.slice_in_dim(block, 0, width, axis=dim), axis, backward)
        block = jnp.concatenate([low, block, high], axis=dim)
    return block


def unit_rows(values):
    mean_square = jnp.mean(values * values, axis=-1, keepdims=True)
    return values * lax.rsqrt(mean_square + 1e-05)


def filter_points(measured, background):
    centered = measured - background
    centered = centered - jnp.mean(centered, axis=-1, keepdims=True)
    return unit_rows(centered).astype(jnp.bfloat16)


def shards(patterns, background, templates, grain_id, keep_mask, grain_row):
    tile_rows, tile_cols, pixels = patterns.shape
    centered_panel = templates.astype(jnp.float32)
    centered_panel = centered_panel - jnp.mean(centered_panel, axis=-1, keepdims=True)
    unit_panel = unit_rows(centered_panel).astype(jnp.bfloat16)
    panels = lax.all_gather(unit_panel, "dict", axis=0, tiled=True)
    patterns, unit_panel = lax.optimization_barrier((patterns, unit_panel))
    filtered = filter_points(patterns, background)
    padded = with_halo(filtered, (("dict", 1), ("scan", 0)), 1)
    neighbour = jnp.zeros((tile_rows, tile_cols, pixels), jnp.float32)
    for row_shift in range(3):
        for col_shift in range(3):
            neighbour = neighbour + padded[
                row_shift : row_shift + tile_rows, col_shift : col_shift + tile_cols
            ].astype(jnp.float32)
    indexed = unit_rows(neighbour).astype(jnp.bfloat16).reshape(tile_rows * tile_cols, pixels)
    point_grain = grain_id.reshape(-1)
    point_keep = keep_mask.reshape(-1)
    grain_count = grain_row.shape[0]
    grain_index = jnp.arange(grain_count, dtype=jnp.int32)
    matches = point_grain[:, None] == grain_index[None, :]
    point_row = jnp.sum(jnp.where(matches, grain_row[None, :], 0), axis=1)
    selector = ((point_row[:, None] == grain_index[None, :]) & (point_keep[:, None] == 1)).astype(
        jnp.bfloat16
    )
    partial_rows = lax.dot_general(
        selector, indexed, (((0,), (0,)), ((), ())), preferred_element_type=jnp.float32
    ).astype(jnp.bfloat16)
    owners = lax.axis_size("scan")
    owned = grain_count // owners
    parts = lax.all_to_all(partial_rows.reshape(owners, owned, pixels), "scan", 0, 0, tiled=True)
    group_total = jnp.sum(parts.astype(jnp.float32), axis=0).astype(jnp.bfloat16)
    group_totals = lax.all_gather(group_total, "dict", axis=0, tiled=False)
    grain_total = jnp.sum(group_totals.astype(jnp.float32), axis=0)
    grain_patterns = unit_rows(grain_total)
    panels, grain_patterns = lax.optimization_barrier((panels, grain_patterns))
    scores = lax.dot_general(
        indexed, panels, (((1,), (1,)), ((), ())), preferred_element_type=jnp.float32
    )
    root_inverse = 1.0 / math.sqrt(pixels)
    max_score = (jnp.max(scores, axis=1) * root_inverse).reshape(tile_rows, tile_cols)
    return (max_score, grain_patterns)


def solution(mesh):
    return jax.shard_map(
        shards,
        mesh=mesh,
        in_specs=(
            P("scan", "dict", None),
            P(),
            P("dict", None),
            P("scan", "dict"),
            P("scan", "dict"),
            P(),
        ),
        out_specs=(P("scan", "dict"), P("scan", None)),
        check_vma=False,
    )
```

```python
import math

import jax
import jax.numpy as jnp
from jax import lax
from jax.experimental import pallas as pl
from jax.experimental.pallas import tpu as pltpu
from jax.sharding import Mesh
from jax.sharding import PartitionSpec as P

SCAN = ("x", "y")
DICT = ("z", "core")
EVERY = ("z", "core", "x", "y")
EPS = 1e-05
VMEM = pltpu.VMEM


def normalise_templates(panel_ref, out_ref, whole_ref):
    panel = panel_ref[...].astype(jnp.float32)
    pixels = panel.shape[0]
    panel = panel - jnp.sum(panel, axis=0, keepdims=True) * (1.0 / pixels)
    mean_square = jnp.sum(panel * panel, axis=0, keepdims=True) * (1.0 / pixels)
    panel = panel * lax.rsqrt(mean_square + EPS)
    whole_ref[...] = panel.T.astype(jnp.bfloat16)
    held = out_ref.shape[0]
    parity = (lax.axis_index("x") + lax.axis_index("y")) & 1
    out_ref[...] = whole_ref[pl.ds(pl.multiple_of(parity * held, held), held), :]


def filter_tile(background_ref, tile_ref, out_ref, low_ref, high_ref, low, high):
    background = background_ref[...]
    rows, _, pixels = tile_ref.shape
    for row in range(rows):
        values = tile_ref[row] - background
        values = values - jnp.sum(values, axis=-1, keepdims=True) * (1.0 / pixels)
        mean_square = jnp.sum(values * values, axis=-1, keepdims=True) * (1.0 / pixels)
        values = (values * lax.rsqrt(mean_square + EPS)).astype(jnp.bfloat16)
        out_ref[row] = values
        low[row : row + 1, :] = values[:1].astype(jnp.float32)
        high[row : row + 1, :] = values[-1:].astype(jnp.float32)
    low_ref[...] = low[...].astype(jnp.bfloat16)
    high_ref[...] = high[...].astype(jnp.bfloat16)


def neighbour_sums(
    point_row_ref, tile_ref, low_ref, high_ref, above_ref, below_ref, out_ref, sums_ref, low_pad, high_pad, shift, ends
):
    rows, cols, pixels = tile_ref.shape
    above, below = above_ref[...].astype(jnp.float32), below_ref[...].astype(jnp.float32)
    for pad, side_ref, corner in ((low_pad, low_ref, cols), (high_pad, high_ref, cols + 1)):
        pad[0:1, :] = above[corner : corner + 1]
        pad[1 : rows + 1, :] = side_ref[...].astype(jnp.float32)
        pad[rows + 1 : rows + 2, :] = below[corner : corner + 1]

    for row in range(rows):
        for side, pad in enumerate((low_pad, high_pad)):
            ends[row, side : side + 1, :] = pad[row : row + 1, :] + pad[row + 1 : row + 2, :] + pad[row + 2 : row + 3, :]

    def one_row(row, before, middle, after):
        column = before + middle + after
        shift[7:8, :] = ends[row, 0:1, :]
        shift[8 : 8 + cols, :] = column
        shift[8 + cols : 9 + cols, :] = ends[row, 1:2, :]
        total = column + shift[7 : 7 + cols, :] + shift[9 : 9 + cols, :]
        mean_square = jnp.sum(total * total, axis=-1, keepdims=True) * (1.0 / pixels)
        values = (total * lax.rsqrt(mean_square + EPS)).astype(jnp.bfloat16)
        out_ref[pl.ds(pl.multiple_of(row * cols, cols), cols), :] = values

    def line(row):
        return tile_ref[row].astype(jnp.float32)

    one_row(0, above[:cols], line(0), line(1))

    def inner(row, carry):
        one_row(row, line(row - 1), line(row), line(row + 1))
        return carry

    lax.fori_loop(1, rows - 1, inner, 0)
    one_row(rows - 1, line(rows - 2), line(rows - 1), below[:cols])
    grains = sums_ref.shape[0]
    k = lax.broadcasted_iota(jnp.int32, (grains, rows * cols), 0)
    half = grains // 2
    grain = (k % half) // 2 * 4 + k // half * 2 + k % 2
    selector = jnp.where(grain == point_row_ref[...], 1.0, 0.0).astype(jnp.bfloat16)
    step = 1024
    for start in range(0, pixels, step):
        stop = min(start + step, pixels)
        sums_ref[:, start:stop] = jnp.dot(
            selector, out_ref[:, start:stop], preferred_element_type=jnp.float32
        ).astype(jnp.bfloat16)


def best_scores(own_ref, other_ref, panel_ref, own_best_ref, other_best_ref):
    first = pl.program_id(0) == 0
    for points_ref, best_ref in ((own_ref, own_best_ref), (other_ref, other_best_ref)):
        scores = lax.dot_general(
            panel_ref[...],
            points_ref[...],
            (((1,), (1,)), ((), ())),
            preferred_element_type=jnp.float32,
        )
        best = jnp.max(scores, axis=0, keepdims=True)

        @pl.when(first)
        def _(best=best, best_ref=best_ref):
            best_ref[...] = best

        @pl.when(jnp.logical_not(first))
        def _(best=best, best_ref=best_ref):
            best_ref[...] = jnp.maximum(best_ref[...], best)


def params(mebibytes):
    return pltpu.CompilerParams(vmem_limit_bytes=mebibytes << 20)


def shards(patterns, background, templates, grain_id, keep_mask, grain_row):
    tile_rows, tile_cols, pixels = patterns.shape
    points = tile_rows * tile_cols
    held = templates.shape[0] // 2
    bf16, f32 = jnp.bfloat16, jnp.float32

    panel = pl.pallas_call(
        normalise_templates,
        out_shape=jax.ShapeDtypeStruct((held, pixels), bf16),
        in_specs=[pl.BlockSpec(memory_space=VMEM)],
        out_specs=pl.BlockSpec(memory_space=VMEM),
        scratch_shapes=[VMEM((2 * held, pixels), bf16)],
        compiler_params=params(10),
        name="normalise_templates",
    )(templates.T)
    panels = lax.all_gather(panel, DICT, axis=0, tiled=True)

    background, panel = lax.optimization_barrier((background, panel))
    block = 8
    filtered, low_edge, high_edge = pl.pallas_call(
        filter_tile,
        grid=(tile_rows // block,),
        out_shape=(
            jax.ShapeDtypeStruct((tile_rows, tile_cols, pixels), bf16),
            jax.ShapeDtypeStruct((tile_rows, pixels), bf16),
            jax.ShapeDtypeStruct((tile_rows, pixels), bf16),
        ),
        in_specs=[
            pl.BlockSpec((1, pixels), lambda i: (0, 0)),
            pl.BlockSpec((block, tile_cols, pixels), lambda i: (i, 0, 0)),
        ],
        out_specs=(
            pl.BlockSpec((block, tile_cols, pixels), lambda i: (i, 0, 0)),
            pl.BlockSpec((block, pixels), lambda i: (i, 0)),
            pl.BlockSpec((block, pixels), lambda i: (i, 0)),
        ),
        scratch_shapes=[VMEM((block, pixels), f32)] * 2,
        compiler_params=params(56),
        name="filter_tile",
    )(background.reshape(1, pixels), patterns)
    columns = lax.axis_size(DICT)
    forward = [(i, i + 1) for i in range(columns - 1)]
    backward = [(i + 1, i) for i in range(columns - 1)]
    low = lax.ppermute(high_edge, DICT, forward)
    high = lax.ppermute(low_edge, DICT, backward)

    def strip(row):
        return jnp.concatenate([filtered[row], low[row : row + 1], high[row : row + 1]], axis=0)

    lines = lax.axis_size(SCAN)
    forward = [(i, i + 1) for i in range(lines - 1)]
    backward = [(i + 1, i) for i in range(lines - 1)]
    above = lax.ppermute(strip(tile_rows - 1), SCAN, forward)
    below = lax.ppermute(strip(0), SCAN, backward)

    grain_count = grain_row.shape[0]
    grain_index = jnp.arange(grain_count, dtype=jnp.int32)
    matches = grain_id.reshape(-1)[:, None] == grain_index[None, :]
    point_row = jnp.sum(jnp.where(matches, grain_row[None, :], 0), axis=1)
    point_row = jnp.where(keep_mask.reshape(-1) == 1, point_row, -1).reshape(1, points)

    indexed, sums = pl.pallas_call(
        neighbour_sums,
        out_shape=(
            jax.ShapeDtypeStruct((points, pixels), bf16),
            jax.ShapeDtypeStruct((grain_count, pixels), bf16),
        ),
        in_specs=[pl.BlockSpec(memory_space=VMEM)] * 6,
        out_specs=[pl.BlockSpec(memory_space=VMEM)] * 2,
        scratch_shapes=[VMEM((24, pixels), f32)] * 2
        + [VMEM((32, pixels), f32), VMEM((tile_rows, 2, pixels), f32)],
        compiler_params=params(12),
        name="neighbour_sums",
    )(point_row, filtered, low, high, above, below)

    xs, ys = lax.axis_size("x"), lax.axis_size("y")
    trade = []
    for z in range(lax.axis_size("z")):
        for x in range(xs):
            for y in range(ys):
                at = z * 2 * xs * ys
                trade.append((at + x * ys + y, at + (x ^ 1) * ys + y))
                trade.append((at + xs * ys + x * ys + y, at + xs * ys + x * ys + (y ^ 1)))
    other = lax.ppermute(indexed.reshape(patterns.shape), EVERY, trade).reshape(points, pixels)

    halves = lax.all_to_all(
        sums.reshape(2, grain_count // 2, pixels), "core", 0, 0, tiled=True
    )
    chip_sums = jnp.sum(halves.astype(f32), axis=0).astype(bf16)
    parts = lax.all_to_all(chip_sums.reshape(lines, -1, pixels), SCAN, 0, 0, tiled=True)
    group_total = jnp.sum(parts.astype(f32), axis=0).astype(bf16)

    block = 256
    scored, group_total = lax.optimization_barrier((other, group_total))
    own_best, other_best = pl.pallas_call(
        best_scores,
        grid=(panels.shape[0] // block,),
        out_shape=(jax.ShapeDtypeStruct((1, points), f32),) * 2,
        in_specs=[
            pl.BlockSpec((points, pixels), lambda i: (0, 0)),
            pl.BlockSpec((points, pixels), lambda i: (0, 0)),
            pl.BlockSpec((block, pixels), lambda i: (i, 0)),
        ],
        out_specs=(pl.BlockSpec((1, points), lambda i: (0, 0)),) * 2,
        compiler_params=params(56),
        name="best_scores",
    )(indexed, scored, panels)
    returned = lax.ppermute(other_best, EVERY, trade)
    other_best, group_total = lax.optimization_barrier((other_best, group_total))
    group_totals = lax.all_gather(group_total, DICT, axis=0, tiled=False)
    returned, group_totals = lax.optimization_barrier((returned, group_totals))
    zs = lax.axis_size("z")
    group_totals = group_totals.reshape((zs, 2) + group_total.shape).astype(f32)
    grain_total = jnp.sum(group_totals, axis=0).reshape(-1, pixels)
    mean_square = jnp.mean(grain_total * grain_total, axis=-1, keepdims=True)
    grain_patterns = grain_total * lax.rsqrt(mean_square + EPS)
    best = jnp.maximum(own_best, returned)
    max_score = (best * (1.0 / math.sqrt(pixels))).reshape(tile_rows, tile_cols)
    return (max_score, grain_patterns)


def solution(mesh):
    groups, lines = mesh.shape["dict"], mesh.shape["scan"]
    fine = Mesh(mesh.devices.reshape(groups // 2, 2, lines // 8, 8), EVERY)
    return jax.shard_map(
        shards,
        mesh=fine,
        in_specs=(
            P(SCAN, DICT, None),
            P(),
            P(DICT, None),
            P(SCAN, DICT),
            P(SCAN, DICT),
            P(),
        ),
        out_specs=(P(SCAN, DICT), P(SCAN, None)),
        check_vma=False,
    )
```

```python
import math

import jax
import jax.numpy as jnp
from jax import lax
from jax.experimental import pallas as pl
from jax.experimental.pallas import tpu as pltpu
from jax.sharding import Mesh
from jax.sharding import PartitionSpec as P

SCAN = ("x", "y")
DICT = ("z", "core")
EVERY = ("z", "core", "x", "y")
EPS = 1e-05
VMEM = pltpu.VMEM


def normalise_templates(panel_ref, out_ref, whole_ref):
    panel = panel_ref[...].astype(jnp.float32)
    pixels = panel.shape[0]
    panel = panel - jnp.sum(panel, axis=0, keepdims=True) * (1.0 / pixels)
    mean_square = jnp.sum(panel * panel, axis=0, keepdims=True) * (1.0 / pixels)
    panel = panel * lax.rsqrt(mean_square + EPS)
    whole_ref[...] = panel.T.astype(jnp.bfloat16)
    held = out_ref.shape[0]
    parity = lax.axis_index("x") & 1
    out_ref[...] = whole_ref[pl.ds(pl.multiple_of(parity * held, held), held), :]


def filter_tile(background_ref, tile_ref, out_ref, low_ref, high_ref, low, high):
    background = background_ref[...].reshape(1, -1)
    rows, _, pixels = tile_ref.shape
    for row in range(rows):
        values = tile_ref[row] - background
        values = values - jnp.sum(values, axis=-1, keepdims=True) * (1.0 / pixels)
        mean_square = jnp.sum(values * values, axis=-1, keepdims=True) * (1.0 / pixels)
        values = (values * lax.rsqrt(mean_square + EPS)).astype(jnp.bfloat16)
        out_ref[row] = values
        low[row : row + 1, :] = values[:1].astype(jnp.float32)
        high[row : row + 1, :] = values[-1:].astype(jnp.float32)
    low_ref[...] = low[...].astype(jnp.bfloat16)
    high_ref[...] = high[...].astype(jnp.bfloat16)


def neighbour_sums(
    point_row_ref, tile_ref, low_ref, high_ref, above_ref, below_ref, out_ref, sums_ref, low_pad, high_pad, shift, ends
):
    rows, cols, pixels = tile_ref.shape
    above, below = above_ref[...].astype(jnp.float32), below_ref[...].astype(jnp.float32)
    for pad, side_ref, corner in ((low_pad, low_ref, cols), (high_pad, high_ref, cols + 1)):
        pad[0:1, :] = above[corner : corner + 1]
        pad[1 : rows + 1, :] = side_ref[...].astype(jnp.float32)
        pad[rows + 1 : rows + 2, :] = below[corner : corner + 1]

    for row in range(rows):
        for side, pad in enumerate((low_pad, high_pad)):
            ends[row, side : side + 1, :] = pad[row : row + 1, :] + pad[row + 1 : row + 2, :] + pad[row + 2 : row + 3, :]

    def one_row(row, before, middle, after):
        column = before + middle + after
        shift[7:8, :] = ends[row, 0:1, :]
        shift[8 : 8 + cols, :] = column
        shift[8 + cols : 9 + cols, :] = ends[row, 1:2, :]
        total = column + shift[7 : 7 + cols, :] + shift[9 : 9 + cols, :]
        mean_square = jnp.sum(total * total, axis=-1, keepdims=True) * (1.0 / pixels)
        values = (total * lax.rsqrt(mean_square + EPS)).astype(jnp.bfloat16)
        out_ref[pl.ds(pl.multiple_of(row * cols, cols), cols), :] = values

    def line(row):
        return tile_ref[row].astype(jnp.float32)

    one_row(0, above[:cols], line(0), line(1))

    def inner(row, carry):
        one_row(row, line(row - 1), line(row), line(row + 1))
        return carry

    lax.fori_loop(1, rows - 1, inner, 0)
    one_row(rows - 1, line(rows - 2), line(rows - 1), below[:cols])
    grains = sums_ref.shape[0]
    k = lax.broadcasted_iota(jnp.int32, (grains, rows * cols), 0)
    half = grains // 2
    grain = (k % half) // 2 * 4 + k // half * 2 + k % 2
    selector = jnp.where(grain == point_row_ref[...], 1.0, 0.0).astype(jnp.bfloat16)
    step = 1024
    for start in range(0, pixels, step):
        stop = min(start + step, pixels)
        sums_ref[:, start:stop] = jnp.dot(
            selector, out_ref[:, start:stop], preferred_element_type=jnp.float32
        ).astype(jnp.bfloat16)


def best_scores(own_ref, other_ref, panel_ref, own_best_ref, other_best_ref, points_ref, best_ref):
    points = own_ref.shape[0]
    step = pl.program_id(0)

    @pl.when(step == 0)
    def _():
        points_ref[:points, :] = own_ref[...]
        points_ref[points:, :] = other_ref[...]
        best_ref[...] = jnp.full(best_ref.shape, -jnp.inf, jnp.float32)

    scores = lax.dot_general(
        points_ref[...], panel_ref[...], (((1,), (1,)), ((), ())), preferred_element_type=jnp.float32
    )
    lanes = best_ref.shape[1]
    best = best_ref[...]
    for start in range(0, scores.shape[1], lanes):
        best = jnp.maximum(best, scores[:, start : start + lanes])
    best_ref[...] = best

    @pl.when(step == pl.num_programs(0) - 1)
    def _():
        best = jnp.max(best_ref[...].T, axis=0, keepdims=True)
        own_best_ref[...] = best[:, :points]
        other_best_ref[...] = best[:, points:]


def finish(own_best_ref, returned_ref, totals_ref, max_score_ref, patterns_ref):
    pixels = patterns_ref.shape[1]
    rows, cols = max_score_ref.shape
    best = jnp.maximum(own_best_ref[...], returned_ref[...]) * (1.0 / math.sqrt(pixels))
    for row in range(rows):
        max_score_ref[row : row + 1, :] = best[:, row * cols : (row + 1) * cols]
    groups = totals_ref.shape[0] // 2
    for core in range(2):
        total = totals_ref[core].astype(jnp.float32)
        for group in range(1, groups):
            total = total + totals_ref[2 * group + core].astype(jnp.float32)
        mean_square = jnp.sum(total * total, axis=-1, keepdims=True) * (1.0 / pixels)
        patterns_ref[2 * core : 2 * core + 2, :] = total * lax.rsqrt(mean_square + EPS)


def params(mebibytes):
    return pltpu.CompilerParams(vmem_limit_bytes=mebibytes << 20)


def shards(patterns, background, templates, grain_id, keep_mask, grain_row):
    tile_rows, tile_cols, pixels = patterns.shape
    points = tile_rows * tile_cols
    held = templates.shape[0] // 2
    bf16, f32 = jnp.bfloat16, jnp.float32

    panel = pl.pallas_call(
        normalise_templates,
        out_shape=jax.ShapeDtypeStruct((held, pixels), bf16),
        in_specs=[pl.BlockSpec(memory_space=VMEM)],
        out_specs=pl.BlockSpec(memory_space=VMEM),
        scratch_shapes=[VMEM((2 * held, pixels), bf16)],
        compiler_params=params(10),
        name="normalise_templates",
    )(templates.T)
    panels = lax.all_gather(panel, DICT, axis=0, tiled=True)

    patterns, panel = lax.optimization_barrier((patterns, panel))
    block = 8
    filtered, low_edge, high_edge = pl.pallas_call(
        filter_tile,
        grid=(tile_rows // block,),
        out_shape=(
            jax.ShapeDtypeStruct((tile_rows, tile_cols, pixels), bf16),
            jax.ShapeDtypeStruct((tile_rows, pixels), bf16),
            jax.ShapeDtypeStruct((tile_rows, pixels), bf16),
        ),
        in_specs=[
            pl.BlockSpec((pixels,), lambda i: (0,)),
            pl.BlockSpec((block, tile_cols, pixels), lambda i: (i, 0, 0)),
        ],
        out_specs=(
            pl.BlockSpec((block, tile_cols, pixels), lambda i: (i, 0, 0)),
            pl.BlockSpec((block, pixels), lambda i: (i, 0)),
            pl.BlockSpec((block, pixels), lambda i: (i, 0)),
        ),
        scratch_shapes=[VMEM((block, pixels), f32)] * 2,
        compiler_params=params(16),
        name="filter_tile",
    )(background, pltpu.with_memory_space_constraint(patterns, pltpu.HBM))
    columns = lax.axis_size(DICT)
    forward = [(i, i + 1) for i in range(columns - 1)]
    backward = [(i + 1, i) for i in range(columns - 1)]
    low = lax.ppermute(high_edge, DICT, forward)
    high = lax.ppermute(low_edge, DICT, backward)

    def strip(row):
        return jnp.concatenate([filtered[row], low[row : row + 1], high[row : row + 1]], axis=0)

    lines = lax.axis_size(SCAN)
    forward = [(i, i + 1) for i in range(lines - 1)]
    backward = [(i + 1, i) for i in range(lines - 1)]
    above = lax.ppermute(strip(tile_rows - 1), SCAN, forward)
    below = lax.ppermute(strip(0), SCAN, backward)

    grain_count = grain_row.shape[0]
    grain_index = jnp.arange(grain_count, dtype=jnp.int32)
    matches = grain_id.reshape(-1)[:, None] == grain_index[None, :]
    point_row = jnp.sum(jnp.where(matches, grain_row[None, :], 0), axis=1)
    point_row = jnp.where(keep_mask.reshape(-1) == 1, point_row, -1).reshape(1, points)

    indexed, sums = pl.pallas_call(
        neighbour_sums,
        out_shape=(
            jax.ShapeDtypeStruct((points, pixels), bf16),
            jax.ShapeDtypeStruct((grain_count, pixels), bf16),
        ),
        in_specs=[pl.BlockSpec(memory_space=VMEM)] * 6,
        out_specs=[pl.BlockSpec(memory_space=VMEM)] * 2,
        scratch_shapes=[VMEM((24, pixels), f32)] * 2
        + [VMEM((32, pixels), f32), VMEM((tile_rows, 2, pixels), f32)],
        compiler_params=params(12),
        name="neighbour_sums",
    )(point_row, filtered, low, high, above, below)

    xs, ys = lax.axis_size("x"), lax.axis_size("y")
    trade = []
    for z in range(lax.axis_size("z")):
        for x in range(xs):
            for y in range(ys):
                for core in range(2):
                    at = (z * 2 + core) * xs
                    partner = (((x + core) ^ 1) - core) % xs
                    trade.append(((at + x) * ys + y, (at + partner) * ys + y))
    other = lax.ppermute(indexed.reshape(patterns.shape), EVERY, trade).reshape(points, pixels)

    halves = lax.all_to_all(
        sums.reshape(2, grain_count // 2, pixels), "core", 0, 0, tiled=True
    )
    chip_sums = jnp.sum(halves.astype(f32), axis=0).astype(bf16)
    parts = lax.all_to_all(chip_sums.reshape(lines, -1, pixels), SCAN, 0, 0, tiled=True)
    group_total = jnp.sum(parts.astype(f32), axis=0).astype(bf16)

    block = 512
    scored, group_total = lax.optimization_barrier((other, group_total))
    own_best, other_best = pl.pallas_call(
        best_scores,
        grid=(panels.shape[0] // block,),
        out_shape=(jax.ShapeDtypeStruct((1, points), f32),) * 2,
        in_specs=[
            pl.BlockSpec((points, pixels), lambda i: (0, 0)),
            pl.BlockSpec((points, pixels), lambda i: (0, 0)),
            pl.BlockSpec((block, pixels), lambda i: (i, 0)),
        ],
        out_specs=(pl.BlockSpec((1, points), lambda i: (0, 0)),) * 2,
        scratch_shapes=[VMEM((2 * points, pixels), bf16), VMEM((2 * points, 128), f32)],
        compiler_params=params(40),
        name="best_scores",
    )(indexed, scored, pltpu.with_memory_space_constraint(panels, pltpu.HBM))
    returned = lax.ppermute(other_best, EVERY, trade)
    other_best, group_total = lax.optimization_barrier((other_best, group_total))
    group_totals = lax.all_gather(group_total, DICT, axis=0, tiled=False)
    returned, group_totals = lax.optimization_barrier((returned, group_totals))
    return pl.pallas_call(
        finish,
        out_shape=(
            jax.ShapeDtypeStruct((tile_rows, tile_cols), f32),
            jax.ShapeDtypeStruct((2 * group_total.shape[0], pixels), f32),
        ),
        in_specs=[pl.BlockSpec(memory_space=VMEM)] * 3,
        out_specs=[pl.BlockSpec(memory_space=VMEM)] * 2,
        compiler_params=params(8),
        name="finish",
    )(own_best, returned, group_totals)


def solution(mesh):
    groups, lines = mesh.shape["dict"], mesh.shape["scan"]
    fine = Mesh(mesh.devices.reshape(groups // 2, 2, lines // 8, 8), EVERY)
    return jax.shard_map(
        shards,
        mesh=fine,
        in_specs=(
            P(SCAN, DICT, None),
            P(),
            P(DICT, None),
            P(SCAN, DICT),
            P(SCAN, DICT),
            P(),
        ),
        out_specs=(P(SCAN, DICT), P(SCAN, None)),
        check_vma=False,
    )
```

```python
import math

import jax
import jax.numpy as jnp
from jax import lax
from jax.experimental import pallas as pl
from jax.experimental.pallas import tpu as pltpu
from jax.sharding import Mesh
from jax.sharding import PartitionSpec as P

SCAN = ("x", "y")
DICT = ("z", "core")
EVERY = ("z", "core", "x", "y")
EPS = 1e-05
VMEM = pltpu.VMEM


def normalise_templates(panel_hbm, out_ref, panel_ref, arrived):
    pixels, lanes = panel_ref.shape
    held = out_ref.shape[0]
    step = pixels // arrived.shape[0]
    copies = []
    for part in range(arrived.shape[0]):
        rows = pl.ds(part * step, step)
        copies.append(pltpu.make_async_copy(panel_hbm.at[rows], panel_ref.at[rows], arrived.at[part]))
        copies[-1].start()
    total = jnp.zeros((1, lanes), jnp.float32)
    for part, copy in enumerate(copies):
        copy.wait()
        values = panel_ref[part * step : (part + 1) * step, :].astype(jnp.float32)
        total = total + jnp.sum(values, axis=0, keepdims=True)
    mean = total * (1.0 / pixels)
    total = jnp.zeros((1, lanes), jnp.float32)
    for start in range(0, pixels, step):
        values = panel_ref[start : start + step, :].astype(jnp.float32) - mean
        total = total + jnp.sum(values * values, axis=0, keepdims=True)
    scale = lax.rsqrt(total * (1.0 / pixels) + EPS)
    first = (lax.axis_index("x") & 1) * held
    lane = lax.broadcasted_iota(jnp.int32, (held, lanes), 1)
    place = lax.broadcasted_iota(jnp.int32, (held, lanes), 0)
    chosen = jnp.where(lane == place + first, 1.0, 0.0).astype(jnp.bfloat16)
    step = 768
    for start in range(0, pixels, step):
        stop = min(start + step, pixels)
        values = (panel_ref[start:stop, :].astype(jnp.float32) - mean) * scale
        out_ref[:, start:stop] = lax.dot_general(
            chosen,
            values.astype(jnp.bfloat16),
            (((1,), (1,)), ((), ())),
            preferred_element_type=jnp.float32,
        ).astype(jnp.bfloat16)


def filter_tile(background_ref, tile_hbm, out_ref, low_ref, high_ref, tile_ref, low, high, arrived):
    rows, cols, pixels = tile_ref.shape
    parts = arrived.shape[0]
    step = rows // parts
    copies = []
    for part in range(parts):
        lines = pl.ds(part * step, step)
        copies.append(pltpu.make_async_copy(tile_hbm.at[lines], tile_ref.at[lines], arrived.at[part]))
        copies[-1].start()
    background = background_ref[...].reshape(1, -1)
    for row in range(rows):
        if row % step == 0:
            copies[row // step].wait()
        values = tile_ref[row] - background
        values = values - jnp.sum(values, axis=-1, keepdims=True) * (1.0 / pixels)
        mean_square = jnp.sum(values * values, axis=-1, keepdims=True) * (1.0 / pixels)
        values = (values * lax.rsqrt(mean_square + EPS)).astype(jnp.bfloat16)
        out_ref[row] = values
        low[row : row + 1, :] = values[:1].astype(jnp.float32)
        high[row : row + 1, :] = values[-1:].astype(jnp.float32)
    low_ref[...] = low[...].astype(jnp.bfloat16)
    high_ref[...] = high[...].astype(jnp.bfloat16)


def index_points(column, low, high, shift):
    cols, pixels = column.shape
    shift[7:8, :] = low
    shift[8 : 8 + cols, :] = column
    shift[8 + cols : 9 + cols, :] = high
    total = column + shift[7 : 7 + cols, :] + shift[9 : 9 + cols, :]
    mean_square = jnp.sum(total * total, axis=-1, keepdims=True) * (1.0 / pixels)
    return (total * lax.rsqrt(mean_square + EPS)).astype(jnp.bfloat16)


def inner_rows(tile_ref, low_ref, high_ref, out_ref, low_pad, high_pad, shift, ends):
    rows, cols, pixels = tile_ref.shape
    for side, (pad, side_ref) in enumerate(((low_pad, low_ref), (high_pad, high_ref))):
        pad[...] = side_ref[...].astype(jnp.float32)
        for row in range(1, rows - 1):
            ends[row, side : side + 1, :] = (
                pad[row - 1 : row, :] + pad[row : row + 1, :] + pad[row + 1 : row + 2, :]
            )

    def line(row):
        return tile_ref[row].astype(jnp.float32)

    def one_row(row, carry):
        column = line(row - 1) + line(row) + line(row + 1)
        start = pl.multiple_of((row - 1) * cols, cols)
        out_ref[pl.ds(start, cols), :] = index_points(
            column, ends[row, 0:1, :], ends[row, 1:2, :], shift
        )
        return carry

    lax.fori_loop(1, rows - 1, one_row, 0)


def outer_rows(
    point_row_ref, first_ref, second_ref, third_ref, fourth_ref, low_ref, high_ref, above_ref, below_ref,
    inner_ref, out_ref, sums_ref, shift,
):
    points, pixels = out_ref.shape
    cols = first_ref.shape[0]
    rows = points // cols
    out_ref[cols : points - cols, :] = inner_ref[...]
    low, high = low_ref[...].astype(jnp.float32), high_ref[...].astype(jnp.float32)
    above, below = above_ref[...].astype(jnp.float32), below_ref[...].astype(jnp.float32)
    for halo, near_ref, next_ref, row, inward in (
        (above, first_ref, second_ref, 0, 1),
        (below, fourth_ref, third_ref, rows - 1, -1),
    ):
        column = halo[:cols] + near_ref[...].astype(jnp.float32) + next_ref[...].astype(jnp.float32)
        edges = []
        for side, values in enumerate((low, high)):
            edges.append(
                halo[cols + side : cols + side + 1]
                + values[row : row + 1]
                + values[row + inward : row + inward + 1]
            )
        out_ref[row * cols : (row + 1) * cols, :] = index_points(column, edges[0], edges[1], shift)
    grains = sums_ref.shape[0]
    k = lax.broadcasted_iota(jnp.int32, (grains, points), 0)
    half = grains // 2
    grain = (k % half) // 2 * 4 + k // half * 2 + k % 2
    selector = jnp.where(grain == point_row_ref[...], 1.0, 0.0).astype(jnp.bfloat16)
    step = 1024
    for start in range(0, pixels, step):
        stop = min(start + step, pixels)
        sums_ref[:, start:stop] = jnp.dot(
            selector, out_ref[:, start:stop], preferred_element_type=jnp.float32
        ).astype(jnp.bfloat16)


def best_scores(own_ref, other_ref, panel_ref, own_best_ref, other_best_ref, points_ref, best_ref):
    points = own_ref.shape[0]
    step = pl.program_id(0)

    @pl.when(step == 0)
    def _():
        points_ref[:points, :] = own_ref[...]
        points_ref[points:, :] = other_ref[...]
        best_ref[...] = jnp.full(best_ref.shape, -jnp.inf, jnp.float32)

    scores = lax.dot_general(
        points_ref[...], panel_ref[...], (((1,), (1,)), ((), ())), preferred_element_type=jnp.float32
    )
    lanes = best_ref.shape[1]
    best = best_ref[...]
    for start in range(0, scores.shape[1], lanes):
        best = jnp.maximum(best, scores[:, start : start + lanes])
    best_ref[...] = best

    @pl.when(step == pl.num_programs(0) - 1)
    def _():
        best = jnp.max(best_ref[...].T, axis=0, keepdims=True)
        own_best_ref[...] = best[:, :points]
        other_best_ref[...] = best[:, points:]


def finish(own_best_ref, returned_ref, totals_ref, max_score_ref, patterns_ref):
    pixels = patterns_ref.shape[1]
    rows, cols = max_score_ref.shape
    best = jnp.maximum(own_best_ref[...], returned_ref[...]) * (1.0 / math.sqrt(pixels))
    for row in range(rows):
        max_score_ref[row : row + 1, :] = best[:, row * cols : (row + 1) * cols]
    groups = totals_ref.shape[0] // 2
    for core in range(2):
        total = totals_ref[core].astype(jnp.float32)
        for group in range(1, groups):
            total = total + totals_ref[2 * group + core].astype(jnp.float32)
        mean_square = jnp.sum(total * total, axis=-1, keepdims=True) * (1.0 / pixels)
        patterns_ref[2 * core : 2 * core + 2, :] = total * lax.rsqrt(mean_square + EPS)


def params(mebibytes):
    return pltpu.CompilerParams(vmem_limit_bytes=mebibytes << 20)


def shards(patterns, background, templates, grain_id, keep_mask, grain_row):
    tile_rows, tile_cols, pixels = patterns.shape
    points = tile_rows * tile_cols
    held = templates.shape[0] // 2
    bf16, f32 = jnp.bfloat16, jnp.float32

    panel = pl.pallas_call(
        normalise_templates,
        out_shape=jax.ShapeDtypeStruct((held, pixels), bf16),
        in_specs=[pl.BlockSpec(memory_space=pl.ANY)],
        out_specs=pl.BlockSpec(memory_space=VMEM),
        scratch_shapes=[VMEM((pixels, 2 * held), bf16), pltpu.SemaphoreType.DMA((5,))],
        compiler_params=params(10),
        name="normalise_templates",
    )(pltpu.with_memory_space_constraint(templates.T, pltpu.HBM))
    panels = lax.all_gather(panel, DICT, axis=0, tiled=True)

    patterns, panel = lax.optimization_barrier((patterns, panel))
    filtered, low_edge, high_edge = pl.pallas_call(
        filter_tile,
        out_shape=(
            jax.ShapeDtypeStruct((tile_rows, tile_cols, pixels), bf16),
            jax.ShapeDtypeStruct((tile_rows, pixels), bf16),
            jax.ShapeDtypeStruct((tile_rows, pixels), bf16),
        ),
        in_specs=[pl.BlockSpec(memory_space=VMEM), pl.BlockSpec(memory_space=pl.ANY)],
        out_specs=(pl.BlockSpec(memory_space=VMEM),) * 3,
        scratch_shapes=[
            VMEM((tile_rows, tile_cols, pixels), f32),
            VMEM((tile_rows, pixels), f32),
            VMEM((tile_rows, pixels), f32),
            pltpu.SemaphoreType.DMA((8,)),
        ],
        compiler_params=params(16),
        name="filter_tile",
    )(
        pltpu.with_memory_space_constraint(background, pltpu.HBM),
        pltpu.with_memory_space_constraint(patterns, pltpu.HBM),
    )
    columns = lax.axis_size(DICT)
    forward = [(i, i + 1) for i in range(columns - 1)]
    backward = [(i + 1, i) for i in range(columns - 1)]
    low = lax.ppermute(high_edge, DICT, forward)
    high = lax.ppermute(low_edge, DICT, backward)

    def strip(row):
        return jnp.concatenate([filtered[row], low[row : row + 1], high[row : row + 1]], axis=0)

    lines = lax.axis_size(SCAN)
    forward = [(i, i + 1) for i in range(lines - 1)]
    backward = [(i + 1, i) for i in range(lines - 1)]
    above = lax.ppermute(strip(tile_rows - 1), SCAN, forward)
    below = lax.ppermute(strip(0), SCAN, backward)

    grain_count = grain_row.shape[0]
    grain_index = jnp.arange(grain_count, dtype=jnp.int32)
    matches = grain_id.reshape(-1)[:, None] == grain_index[None, :]
    point_row = jnp.sum(jnp.where(matches, grain_row[None, :], 0), axis=1)
    point_row = jnp.where(keep_mask.reshape(-1) == 1, point_row, -1).reshape(1, points)

    inner_points = points - 2 * tile_cols
    inner = pl.pallas_call(
        inner_rows,
        out_shape=jax.ShapeDtypeStruct((inner_points, pixels), bf16),
        in_specs=[pl.BlockSpec(memory_space=VMEM)] * 3,
        out_specs=pl.BlockSpec(memory_space=VMEM),
        scratch_shapes=[VMEM((tile_rows, pixels), f32)] * 2
        + [VMEM((32, pixels), f32), VMEM((tile_rows, 2, pixels), f32)],
        compiler_params=params(10),
        cost_estimate=pl.CostEstimate(
            flops=12 * inner_points * pixels, bytes_accessed=16 * inner_points * pixels, transcendentals=0
        ),
        name="inner_rows",
    )(filtered, low, high)
    indexed, sums = pl.pallas_call(
        outer_rows,
        out_shape=(
            jax.ShapeDtypeStruct((points, pixels), bf16),
            jax.ShapeDtypeStruct((grain_count, pixels), bf16),
        ),
        in_specs=[pl.BlockSpec(memory_space=VMEM)] * 10,
        out_specs=[pl.BlockSpec(memory_space=VMEM)] * 2,
        scratch_shapes=[VMEM((32, pixels), f32)],
        compiler_params=params(10),
        name="outer_rows",
    )(point_row, filtered[0], filtered[1], filtered[-2], filtered[-1], low, high, above, below, inner)

    xs, ys = lax.axis_size("x"), lax.axis_size("y")
    trade = []
    for z in range(lax.axis_size("z")):
        for x in range(xs):
            for y in range(ys):
                for core in range(2):
                    at = (z * 2 + core) * xs
                    partner = (((x + core) ^ 1) - core) % xs
                    trade.append(((at + x) * ys + y, (at + partner) * ys + y))
    other = lax.ppermute(indexed.reshape(patterns.shape), EVERY, trade).reshape(points, pixels)

    halves = lax.all_to_all(
        sums.reshape(2, grain_count // 2, pixels), "core", 0, 0, tiled=True
    )
    chip_sums = jnp.sum(halves.astype(f32), axis=0).astype(bf16)
    parts = lax.all_to_all(chip_sums.reshape(lines, -1, pixels), SCAN, 0, 0, tiled=True)
    group_total = jnp.sum(parts.astype(f32), axis=0).astype(bf16)

    block = 512
    scored, group_total = lax.optimization_barrier((other, group_total))
    own_best, other_best = pl.pallas_call(
        best_scores,
        grid=(panels.shape[0] // block,),
        out_shape=(jax.ShapeDtypeStruct((1, points), f32),) * 2,
        in_specs=[
            pl.BlockSpec((points, pixels), lambda i: (0, 0)),
            pl.BlockSpec((points, pixels), lambda i: (0, 0)),
            pl.BlockSpec((block, pixels), lambda i: (i, 0)),
        ],
        out_specs=(pl.BlockSpec((1, points), lambda i: (0, 0)),) * 2,
        scratch_shapes=[VMEM((2 * points, pixels), bf16), VMEM((2 * points, 128), f32)],
        compiler_params=params(28),
        name="best_scores",
    )(indexed, scored, pltpu.with_memory_space_constraint(panels, pltpu.HBM))
    returned = lax.ppermute(other_best, EVERY, trade)
    other_best, group_total = lax.optimization_barrier((other_best, group_total))
    group_totals = lax.all_gather(group_total, DICT, axis=0, tiled=False)
    returned, group_totals = lax.optimization_barrier((returned, group_totals))
    return pl.pallas_call(
        finish,
        out_shape=(
            jax.ShapeDtypeStruct((tile_rows, tile_cols), f32),
            jax.ShapeDtypeStruct((2 * group_total.shape[0], pixels), f32),
        ),
        in_specs=[pl.BlockSpec(memory_space=VMEM)] * 3,
        out_specs=[pl.BlockSpec(memory_space=VMEM)] * 2,
        compiler_params=params(8),
        name="finish",
    )(own_best, returned, group_totals)


def solution(mesh):
    groups, lines = mesh.shape["dict"], mesh.shape["scan"]
    fine = Mesh(mesh.devices.reshape(groups // 2, 2, lines // 8, 8), EVERY)
    return jax.shard_map(
        shards,
        mesh=fine,
        in_specs=(
            P(SCAN, DICT, None),
            P(),
            P(DICT, None),
            P(SCAN, DICT),
            P(SCAN, DICT),
            P(),
        ),
        out_specs=(P(SCAN, DICT), P(SCAN, None)),
        check_vma=False,
    )
```

```python
import math

import jax
import jax.numpy as jnp
from jax import lax
from jax.experimental import pallas as pl
from jax.experimental.pallas import tpu as pltpu
from jax.sharding import Mesh
from jax.sharding import PartitionSpec as P

SCAN = ("x", "y")
DICT = ("z", "core")
EVERY = ("z", "core", "x", "y")
EPS = 1e-05
VMEM = pltpu.VMEM


def normalise_templates(panel_hbm, out_ref, panel_ref, arrived):
    pixels, lanes = panel_ref.shape
    held = out_ref.shape[0]
    step = pixels // arrived.shape[0]
    copies = []
    for part in range(arrived.shape[0]):
        rows = pl.ds(part * step, step)
        copies.append(pltpu.make_async_copy(panel_hbm.at[rows], panel_ref.at[rows], arrived.at[part]))
        copies[-1].start()
    total = jnp.zeros((1, lanes), jnp.float32)
    for part, copy in enumerate(copies):
        copy.wait()
        values = panel_ref[part * step : (part + 1) * step, :].astype(jnp.float32)
        total = total + jnp.sum(values, axis=0, keepdims=True)
    mean = total * (1.0 / pixels)
    total = jnp.zeros((1, lanes), jnp.float32)
    for start in range(0, pixels, step):
        values = panel_ref[start : start + step, :].astype(jnp.float32) - mean
        total = total + jnp.sum(values * values, axis=0, keepdims=True)
    scale = lax.rsqrt(total * (1.0 / pixels) + EPS)
    first = (lax.axis_index("x") & 1) * held
    lane = lax.broadcasted_iota(jnp.int32, (held, lanes), 1)
    place = lax.broadcasted_iota(jnp.int32, (held, lanes), 0)
    chosen = jnp.where(lane == place + first, 1.0, 0.0).astype(jnp.bfloat16)
    step = 768
    for start in range(0, pixels, step):
        stop = min(start + step, pixels)
        values = (panel_ref[start:stop, :].astype(jnp.float32) - mean) * scale
        out_ref[:, start:stop] = lax.dot_general(
            chosen,
            values.astype(jnp.bfloat16),
            (((1,), (1,)), ((), ())),
            preferred_element_type=jnp.float32,
        ).astype(jnp.bfloat16)


def filter_tile(background_ref, tile_ref, out_ref, low_ref, high_ref, low, high):
    background = background_ref[...].reshape(1, -1)
    rows, _, pixels = tile_ref.shape
    for row in range(rows):
        values = tile_ref[row] - background
        values = values - jnp.sum(values, axis=-1, keepdims=True) * (1.0 / pixels)
        mean_square = jnp.sum(values * values, axis=-1, keepdims=True) * (1.0 / pixels)
        values = (values * lax.rsqrt(mean_square + EPS)).astype(jnp.bfloat16)
        out_ref[row] = values
        low[row : row + 1, :] = values[:1].astype(jnp.float32)
        high[row : row + 1, :] = values[-1:].astype(jnp.float32)
    low_ref[...] = low[...].astype(jnp.bfloat16)
    high_ref[...] = high[...].astype(jnp.bfloat16)


def index_points(column, low, high, shift):
    cols, pixels = column.shape
    shift[7:8, :] = low
    shift[8 : 8 + cols, :] = column
    shift[8 + cols : 9 + cols, :] = high
    total = column + shift[7 : 7 + cols, :] + shift[9 : 9 + cols, :]
    mean_square = jnp.sum(total * total, axis=-1, keepdims=True) * (1.0 / pixels)
    return (total * lax.rsqrt(mean_square + EPS)).astype(jnp.bfloat16)


def inner_rows(tile_ref, low_ref, high_ref, out_ref, low_pad, high_pad, shift, ends):
    rows, cols, pixels = tile_ref.shape
    for side, (pad, side_ref) in enumerate(((low_pad, low_ref), (high_pad, high_ref))):
        pad[...] = side_ref[...].astype(jnp.float32)
        for row in range(1, rows - 1):
            ends[row, side : side + 1, :] = (
                pad[row - 1 : row, :] + pad[row : row + 1, :] + pad[row + 1 : row + 2, :]
            )

    def line(row):
        return tile_ref[row].astype(jnp.float32)

    def one_row(row, carry):
        column = line(row - 1) + line(row) + line(row + 1)
        start = pl.multiple_of((row - 1) * cols, cols)
        out_ref[pl.ds(start, cols), :] = index_points(
            column, ends[row, 0:1, :], ends[row, 1:2, :], shift
        )
        return carry

    lax.fori_loop(1, rows - 1, one_row, 0)


def outer_rows(
    point_row_ref, first_ref, second_ref, third_ref, fourth_ref, low_ref, high_ref, above_ref, below_ref,
    inner_ref, out_ref, kept_ref, sent_ref, shift,
):
    points, pixels = out_ref.shape
    cols = first_ref.shape[0]
    rows = points // cols
    out_ref[cols : points - cols, :] = inner_ref[...]
    low, high = low_ref[...].astype(jnp.float32), high_ref[...].astype(jnp.float32)
    above, below = above_ref[...].astype(jnp.float32), below_ref[...].astype(jnp.float32)
    for halo, near_ref, next_ref, row, inward in (
        (above, first_ref, second_ref, 0, 1),
        (below, fourth_ref, third_ref, rows - 1, -1),
    ):
        column = halo[:cols] + near_ref[...].astype(jnp.float32) + next_ref[...].astype(jnp.float32)
        edges = []
        for side, values in enumerate((low, high)):
            edges.append(
                halo[cols + side : cols + side + 1]
                + values[row : row + 1]
                + values[row + inward : row + inward + 1]
            )
        out_ref[row * cols : (row + 1) * cols, :] = index_points(column, edges[0], edges[1], shift)
    half = kept_ref.shape[0]
    k = lax.broadcasted_iota(jnp.int32, (2 * half, points), 0)
    core = lax.axis_index("core") ^ (k // half)
    grain = (k % half) // 2 * 4 + core * 2 + k % 2
    selector = jnp.where(grain == point_row_ref[...], 1.0, 0.0).astype(jnp.bfloat16)
    step = 1024
    for start in range(0, pixels, step):
        stop = min(start + step, pixels)
        sums = jnp.dot(selector, out_ref[:, start:stop], preferred_element_type=jnp.float32)
        kept_ref[:, start:stop] = sums[:half]
        sent_ref[:, start:stop] = sums[half:].astype(jnp.bfloat16)


def best_scores(own_ref, other_ref, panel_ref, own_best_ref, other_best_ref, points_ref, best_ref):
    points = own_ref.shape[0]
    step = pl.program_id(0)

    @pl.when(step == 0)
    def _():
        points_ref[:points, :] = own_ref[...]
        points_ref[points:, :] = other_ref[...]
        best_ref[...] = jnp.full(best_ref.shape, -jnp.inf, jnp.float32)

    scores = lax.dot_general(
        points_ref[...], panel_ref[...], (((1,), (1,)), ((), ())), preferred_element_type=jnp.float32
    )
    lanes = best_ref.shape[1]
    best = best_ref[...]
    for start in range(0, scores.shape[1], lanes):
        best = jnp.maximum(best, scores[:, start : start + lanes])
    best_ref[...] = best

    @pl.when(step == pl.num_programs(0) - 1)
    def _():
        best = jnp.max(best_ref[...].T, axis=0, keepdims=True)
        own_best_ref[...] = best[:, :points]
        other_best_ref[...] = best[:, points:]


def finish(own_best_ref, returned_ref, totals_ref, max_score_ref, patterns_ref):
    pixels = patterns_ref.shape[1]
    rows, cols = max_score_ref.shape
    best = jnp.maximum(own_best_ref[...], returned_ref[...]) * (1.0 / math.sqrt(pixels))
    for row in range(rows):
        max_score_ref[row : row + 1, :] = best[:, row * cols : (row + 1) * cols]
    groups = totals_ref.shape[0] // 2
    for core in range(2):
        total = totals_ref[core].astype(jnp.float32)
        for group in range(1, groups):
            total = total + totals_ref[2 * group + core].astype(jnp.float32)
        mean_square = jnp.sum(total * total, axis=-1, keepdims=True) * (1.0 / pixels)
        patterns_ref[2 * core : 2 * core + 2, :] = total * lax.rsqrt(mean_square + EPS)


def params(mebibytes):
    return pltpu.CompilerParams(vmem_limit_bytes=mebibytes << 20)


def shards(patterns, background, templates, grain_id, keep_mask, grain_row):
    tile_rows, tile_cols, pixels = patterns.shape
    points = tile_rows * tile_cols
    held = templates.shape[0] // 2
    bf16, f32 = jnp.bfloat16, jnp.float32

    panel = pl.pallas_call(
        normalise_templates,
        out_shape=jax.ShapeDtypeStruct((held, pixels), bf16),
        in_specs=[pl.BlockSpec(memory_space=pl.ANY)],
        out_specs=pl.BlockSpec(memory_space=VMEM),
        scratch_shapes=[VMEM((pixels, 2 * held), bf16), pltpu.SemaphoreType.DMA((5,))],
        compiler_params=params(10),
        name="normalise_templates",
    )(pltpu.with_memory_space_constraint(templates.T, pltpu.HBM))
    panels = lax.all_gather(panel, DICT, axis=0, tiled=True)

    patterns, panel = lax.optimization_barrier((patterns, panel))
    block = tile_rows // 2
    filtered, low_edge, high_edge = pl.pallas_call(
        filter_tile,
        grid=(tile_rows // block,),
        out_shape=(
            jax.ShapeDtypeStruct((tile_rows, tile_cols, pixels), bf16),
            jax.ShapeDtypeStruct((tile_rows, pixels), bf16),
            jax.ShapeDtypeStruct((tile_rows, pixels), bf16),
        ),
        in_specs=[
            pl.BlockSpec((pixels,), lambda i: (0,)),
            pl.BlockSpec((block, tile_cols, pixels), lambda i: (i, 0, 0)),
        ],
        out_specs=(
            pl.BlockSpec((block, tile_cols, pixels), lambda i: (i, 0, 0)),
            pl.BlockSpec((block, pixels), lambda i: (i, 0)),
            pl.BlockSpec((block, pixels), lambda i: (i, 0)),
        ),
        scratch_shapes=[VMEM((block, pixels), f32)] * 2,
        compiler_params=params(16),
        name="filter_tile",
    )(
        pltpu.with_memory_space_constraint(background, pltpu.HBM),
        pltpu.with_memory_space_constraint(patterns, pltpu.HBM),
    )
    columns = lax.axis_size(DICT)
    forward = [(i, i + 1) for i in range(columns - 1)]
    backward = [(i + 1, i) for i in range(columns - 1)]
    low = lax.ppermute(high_edge, DICT, forward)
    high = lax.ppermute(low_edge, DICT, backward)

    def strip(row):
        return jnp.concatenate([filtered[row], low[row : row + 1], high[row : row + 1]], axis=0)

    lines = lax.axis_size(SCAN)
    forward = [(i, i + 1) for i in range(lines - 1)]
    backward = [(i + 1, i) for i in range(lines - 1)]
    above = lax.ppermute(strip(tile_rows - 1), SCAN, forward)
    below = lax.ppermute(strip(0), SCAN, backward)

    grain_count = grain_row.shape[0]
    grain_index = jnp.arange(grain_count, dtype=jnp.int32)
    matches = grain_id.reshape(-1)[:, None] == grain_index[None, :]
    point_row = jnp.sum(jnp.where(matches, grain_row[None, :], 0), axis=1)
    point_row = jnp.where(keep_mask.reshape(-1) == 1, point_row, -1).reshape(1, points)

    inner_points = points - 2 * tile_cols
    inner = pl.pallas_call(
        inner_rows,
        out_shape=jax.ShapeDtypeStruct((inner_points, pixels), bf16),
        in_specs=[pl.BlockSpec(memory_space=VMEM)] * 3,
        out_specs=pl.BlockSpec(memory_space=VMEM),
        scratch_shapes=[VMEM((tile_rows, pixels), f32)] * 2
        + [VMEM((32, pixels), f32), VMEM((tile_rows, 2, pixels), f32)],
        compiler_params=params(10),
        cost_estimate=pl.CostEstimate(
            flops=12 * inner_points * pixels, bytes_accessed=16 * inner_points * pixels, transcendentals=0
        ),
        name="inner_rows",
    )(filtered, low, high)
    indexed, kept, sent = pl.pallas_call(
        outer_rows,
        out_shape=(
            jax.ShapeDtypeStruct((points, pixels), bf16),
            jax.ShapeDtypeStruct((grain_count // 2, pixels), f32),
            jax.ShapeDtypeStruct((grain_count // 2, pixels), bf16),
        ),
        in_specs=[pl.BlockSpec(memory_space=VMEM)] * 10,
        out_specs=[pl.BlockSpec(memory_space=VMEM)] * 3,
        scratch_shapes=[VMEM((32, pixels), f32)],
        compiler_params=params(10),
        name="outer_rows",
    )(point_row, filtered[0], filtered[1], filtered[-2], filtered[-1], low, high, above, below, inner)

    xs, ys = lax.axis_size("x"), lax.axis_size("y")
    trade = []
    for z in range(lax.axis_size("z")):
        for x in range(xs):
            for y in range(ys):
                for core in range(2):
                    at = (z * 2 + core) * xs
                    partner = (((x + core) ^ 1) - core) % xs
                    trade.append(((at + x) * ys + y, (at + partner) * ys + y))
    swapped = lax.ppermute(sent, "core", [(0, 1), (1, 0)])
    other = lax.ppermute(indexed.reshape(patterns.shape), EVERY, trade).reshape(points, pixels)

    chip_sums = (kept + swapped.astype(f32)).astype(bf16)
    parts = lax.all_to_all(chip_sums.reshape(lines, -1, pixels), SCAN, 0, 0, tiled=True)
    group_total = jnp.sum(parts.astype(f32), axis=0).astype(bf16)

    block = 512
    scored, group_total = lax.optimization_barrier((other, group_total))
    own_best, other_best = pl.pallas_call(
        best_scores,
        grid=(panels.shape[0] // block,),
        out_shape=(jax.ShapeDtypeStruct((1, points), f32),) * 2,
        in_specs=[
            pl.BlockSpec((points, pixels), lambda i: (0, 0)),
            pl.BlockSpec((points, pixels), lambda i: (0, 0)),
            pl.BlockSpec((block, pixels), lambda i: (i, 0)),
        ],
        out_specs=(pl.BlockSpec((1, points), lambda i: (0, 0)),) * 2,
        scratch_shapes=[VMEM((2 * points, pixels), bf16), VMEM((2 * points, 128), f32)],
        compiler_params=params(28),
        name="best_scores",
    )(indexed, scored, pltpu.with_memory_space_constraint(panels, pltpu.HBM))
    returned = lax.ppermute(other_best, EVERY, trade)
    other_best, group_total = lax.optimization_barrier((other_best, group_total))
    group_totals = lax.all_gather(group_total, DICT, axis=0, tiled=False)
    returned, group_totals = lax.optimization_barrier((returned, group_totals))
    return pl.pallas_call(
        finish,
        out_shape=(
            jax.ShapeDtypeStruct((tile_rows, tile_cols), f32),
            jax.ShapeDtypeStruct((2 * group_total.shape[0], pixels), f32),
        ),
        in_specs=[pl.BlockSpec(memory_space=VMEM)] * 3,
        out_specs=[pl.BlockSpec(memory_space=VMEM)] * 2,
        compiler_params=params(8),
        name="finish",
    )(own_best, returned, group_totals)


def solution(mesh):
    groups, lines = mesh.shape["dict"], mesh.shape["scan"]
    fine = Mesh(mesh.devices.reshape(groups // 2, 2, lines // 8, 8), EVERY)
    return jax.shard_map(
        shards,
        mesh=fine,
        in_specs=(
            P(SCAN, DICT, None),
            P(),
            P(DICT, None),
            P(SCAN, DICT),
            P(SCAN, DICT),
            P(),
        ),
        out_specs=(P(SCAN, DICT), P(SCAN, None)),
        check_vma=False,
    )
```

```python
import functools
import math

import jax
import jax.numpy as jnp
from jax import lax
from jax.experimental import pallas as pl
from jax.experimental.pallas import tpu as pltpu
from jax.sharding import Mesh
from jax.sharding import PartitionSpec as P

SCAN = ("x", "y")
DICT = ("z", "core")
EVERY = ("z", "core", "x", "y")
EPS = 1e-05
VMEM = pltpu.VMEM


def normalise_templates(panel_hbm, out_ref, panel_ref, arrived):
    pixels, lanes = panel_ref.shape
    held = out_ref.shape[0]
    step = pixels // arrived.shape[0]
    copies = []
    for part in range(arrived.shape[0]):
        rows = pl.ds(part * step, step)
        copies.append(pltpu.make_async_copy(panel_hbm.at[rows], panel_ref.at[rows], arrived.at[part]))
        copies[-1].start()
    total = jnp.zeros((1, lanes), jnp.float32)
    for part, copy in enumerate(copies):
        copy.wait()
        values = panel_ref[part * step : (part + 1) * step, :].astype(jnp.float32)
        total = total + jnp.sum(values, axis=0, keepdims=True)
    mean = total * (1.0 / pixels)
    total = jnp.zeros((1, lanes), jnp.float32)
    for start in range(0, pixels, step):
        values = panel_ref[start : start + step, :].astype(jnp.float32) - mean
        total = total + jnp.sum(values * values, axis=0, keepdims=True)
    scale = lax.rsqrt(total * (1.0 / pixels) + EPS)
    first = (lax.axis_index("x") & 1) * held
    lane = lax.broadcasted_iota(jnp.int32, (held, lanes), 1)
    place = lax.broadcasted_iota(jnp.int32, (held, lanes), 0)
    chosen = jnp.where(lane == place + first, 1.0, 0.0).astype(jnp.bfloat16)
    step = 768
    for start in range(0, pixels, step):
        stop = min(start + step, pixels)
        values = (panel_ref[start:stop, :].astype(jnp.float32) - mean) * scale
        out_ref[:, start:stop] = lax.dot_general(
            chosen,
            values.astype(jnp.bfloat16),
            (((1,), (1,)), ((), ())),
            preferred_element_type=jnp.float32,
        ).astype(jnp.bfloat16)


def filter_tile(background_ref, tile_ref, out_ref, low_ref, high_ref, low, high):
    background = background_ref[...].reshape(1, -1)
    rows, _, pixels = tile_ref.shape
    for row in range(rows):
        values = tile_ref[row] - background
        values = values - jnp.sum(values, axis=-1, keepdims=True) * (1.0 / pixels)
        mean_square = jnp.sum(values * values, axis=-1, keepdims=True) * (1.0 / pixels)
        values = (values * lax.rsqrt(mean_square + EPS)).astype(jnp.bfloat16)
        out_ref[row] = values
        low[row : row + 1, :] = values[:1].astype(jnp.float32)
        high[row : row + 1, :] = values[-1:].astype(jnp.float32)
    low_ref[...] = low[...].astype(jnp.bfloat16)
    high_ref[...] = high[...].astype(jnp.bfloat16)


def index_points(column, low, high, shift):
    cols, pixels = column.shape
    shift[7:8, :] = low
    shift[8 : 8 + cols, :] = column
    shift[8 + cols : 9 + cols, :] = high
    total = column + shift[7 : 7 + cols, :] + shift[9 : 9 + cols, :]
    mean_square = jnp.sum(total * total, axis=-1, keepdims=True) * (1.0 / pixels)
    return (total * lax.rsqrt(mean_square + EPS)).astype(jnp.bfloat16)


def inner_rows(tile_ref, low_ref, high_ref, out_ref, low_pad, high_pad, shift, ends):
    rows, cols, pixels = tile_ref.shape
    for side, (pad, side_ref) in enumerate(((low_pad, low_ref), (high_pad, high_ref))):
        pad[...] = side_ref[...].astype(jnp.float32)
        for row in range(1, rows - 1):
            ends[row, side : side + 1, :] = (
                pad[row - 1 : row, :] + pad[row : row + 1, :] + pad[row + 1 : row + 2, :]
            )

    def line(row):
        return tile_ref[row].astype(jnp.float32)

    def one_row(row, carry):
        column = line(row - 1) + line(row) + line(row + 1)
        start = pl.multiple_of((row - 1) * cols, cols)
        out_ref[pl.ds(start, cols), :] = index_points(
            column, ends[row, 0:1, :], ends[row, 1:2, :], shift
        )
        return carry

    lax.fori_loop(1, rows - 1, one_row, 0)


def outer_rows(
    point_row_ref, first_ref, second_ref, third_ref, fourth_ref, low_ref, high_ref, above_ref, below_ref,
    inner_ref, out_ref, kept_ref, sent_ref, shift,
):
    points, pixels = out_ref.shape
    cols = first_ref.shape[0]
    rows = points // cols
    out_ref[cols : points - cols, :] = inner_ref[...]
    low, high = low_ref[...].astype(jnp.float32), high_ref[...].astype(jnp.float32)
    above, below = above_ref[...].astype(jnp.float32), below_ref[...].astype(jnp.float32)
    for halo, near_ref, next_ref, row, inward in (
        (above, first_ref, second_ref, 0, 1),
        (below, fourth_ref, third_ref, rows - 1, -1),
    ):
        column = halo[:cols] + near_ref[...].astype(jnp.float32) + next_ref[...].astype(jnp.float32)
        edges = []
        for side, values in enumerate((low, high)):
            edges.append(
                halo[cols + side : cols + side + 1]
                + values[row : row + 1]
                + values[row + inward : row + inward + 1]
            )
        out_ref[row * cols : (row + 1) * cols, :] = index_points(column, edges[0], edges[1], shift)
    half = kept_ref.shape[0]
    k = lax.broadcasted_iota(jnp.int32, (2 * half, points), 0)
    core = lax.axis_index("core") ^ (k // half)
    grain = (k % half) // 2 * 4 + core * 2 + k % 2
    selector = jnp.where(grain == point_row_ref[...], 1.0, 0.0).astype(jnp.bfloat16)
    step = 1024
    for start in range(0, pixels, step):
        stop = min(start + step, pixels)
        sums = jnp.dot(selector, out_ref[:, start:stop], preferred_element_type=jnp.float32)
        kept_ref[:, start:stop] = sums[:half]
        sent_ref[:, start:stop] = sums[half:].astype(jnp.bfloat16)


def lane_best(best, scores):
    lanes = best.shape[1]
    for start in range(0, scores.shape[1], lanes):
        best = jnp.maximum(best, scores[:, start : start + lanes])
    return best


def products(points, panel):
    return lax.dot_general(points, panel, (((1,), (1,)), ((), ())), preferred_element_type=jnp.float32)


def own_scores(points_ref, panel_ref, out_ref, best_ref):
    step = pl.program_id(0)

    @pl.when(step == 0)
    def _():
        best_ref[...] = jnp.full(best_ref.shape, -jnp.inf, jnp.float32)

    best = lane_best(best_ref[...], products(points_ref[...], panel_ref[...]))
    best_ref[...] = best

    @pl.when(step == pl.num_programs(0) - 1)
    def _():
        out_ref[...] = jnp.max(best.T, axis=0, keepdims=True)


def other_scores(points_ref, panel_ref, out_ref):
    points = points_ref[...]
    best = jnp.full((points.shape[0], 128), -jnp.inf, jnp.float32)
    block = 512
    for start in range(0, panel_ref.shape[0], block):
        best = lane_best(best, products(points, panel_ref[start : start + block, :]))
    out_ref[...] = jnp.max(best.T, axis=0, keepdims=True)


def finish_scores(own_best_ref, returned_ref, max_score_ref, pixels):
    rows, cols = max_score_ref.shape
    best = jnp.maximum(own_best_ref[...], returned_ref[...]) * (1.0 / math.sqrt(pixels))
    for row in range(rows):
        max_score_ref[row : row + 1, :] = best[:, row * cols : (row + 1) * cols]


def finish_patterns(totals_ref, patterns_ref):
    pixels = patterns_ref.shape[1]
    groups = totals_ref.shape[0] // 2
    for core in range(2):
        total = totals_ref[core].astype(jnp.float32)
        for group in range(1, groups):
            total = total + totals_ref[2 * group + core].astype(jnp.float32)
        mean_square = jnp.sum(total * total, axis=-1, keepdims=True) * (1.0 / pixels)
        patterns_ref[2 * core : 2 * core + 2, :] = total * lax.rsqrt(mean_square + EPS)


def params(mebibytes):
    return pltpu.CompilerParams(vmem_limit_bytes=mebibytes << 20)


def shards(patterns, background, templates, grain_id, keep_mask, grain_row):
    tile_rows, tile_cols, pixels = patterns.shape
    points = tile_rows * tile_cols
    held = templates.shape[0] // 2
    bf16, f32 = jnp.bfloat16, jnp.float32

    panel = pl.pallas_call(
        normalise_templates,
        out_shape=jax.ShapeDtypeStruct((held, pixels), bf16),
        in_specs=[pl.BlockSpec(memory_space=pl.ANY)],
        out_specs=pl.BlockSpec(memory_space=VMEM),
        scratch_shapes=[VMEM((pixels, 2 * held), bf16), pltpu.SemaphoreType.DMA((5,))],
        compiler_params=params(10),
        name="normalise_templates",
    )(pltpu.with_memory_space_constraint(templates.T, pltpu.HBM))
    panels = lax.all_gather(panel, DICT, axis=0, tiled=True)

    patterns, panel = lax.optimization_barrier((patterns, panel))
    block = tile_rows // 2
    filtered, low_edge, high_edge = pl.pallas_call(
        filter_tile,
        grid=(tile_rows // block,),
        out_shape=(
            jax.ShapeDtypeStruct((tile_rows, tile_cols, pixels), bf16),
            jax.ShapeDtypeStruct((tile_rows, pixels), bf16),
            jax.ShapeDtypeStruct((tile_rows, pixels), bf16),
        ),
        in_specs=[
            pl.BlockSpec((pixels,), lambda i: (0,)),
            pl.BlockSpec((block, tile_cols, pixels), lambda i: (i, 0, 0)),
        ],
        out_specs=(
            pl.BlockSpec((block, tile_cols, pixels), lambda i: (i, 0, 0)),
            pl.BlockSpec((block, pixels), lambda i: (i, 0)),
            pl.BlockSpec((block, pixels), lambda i: (i, 0)),
        ),
        scratch_shapes=[VMEM((block, pixels), f32)] * 2,
        compiler_params=params(16),
        name="filter_tile",
    )(
        pltpu.with_memory_space_constraint(background, pltpu.HBM),
        pltpu.with_memory_space_constraint(patterns, pltpu.HBM),
    )
    columns = lax.axis_size(DICT)
    forward = [(i, i + 1) for i in range(columns - 1)]
    backward = [(i + 1, i) for i in range(columns - 1)]
    low = lax.ppermute(high_edge, DICT, forward)
    high = lax.ppermute(low_edge, DICT, backward)

    def strip(row):
        return jnp.concatenate([filtered[row], low[row : row + 1], high[row : row + 1]], axis=0)

    lines = lax.axis_size(SCAN)
    forward = [(i, i + 1) for i in range(lines - 1)]
    backward = [(i + 1, i) for i in range(lines - 1)]
    above = lax.ppermute(strip(tile_rows - 1), SCAN, forward)
    below = lax.ppermute(strip(0), SCAN, backward)

    grain_count = grain_row.shape[0]
    grain_index = jnp.arange(grain_count, dtype=jnp.int32)
    matches = grain_id.reshape(-1)[:, None] == grain_index[None, :]
    point_row = jnp.sum(jnp.where(matches, grain_row[None, :], 0), axis=1)
    point_row = jnp.where(keep_mask.reshape(-1) == 1, point_row, -1).reshape(1, points)

    inner_points = points - 2 * tile_cols
    inner = pl.pallas_call(
        inner_rows,
        out_shape=jax.ShapeDtypeStruct((inner_points, pixels), bf16),
        in_specs=[pl.BlockSpec(memory_space=VMEM)] * 3,
        out_specs=pl.BlockSpec(memory_space=VMEM),
        scratch_shapes=[VMEM((tile_rows, pixels), f32)] * 2
        + [VMEM((32, pixels), f32), VMEM((tile_rows, 2, pixels), f32)],
        compiler_params=params(10),
        cost_estimate=pl.CostEstimate(
            flops=12 * inner_points * pixels, bytes_accessed=16 * inner_points * pixels, transcendentals=0
        ),
        name="inner_rows",
    )(filtered, low, high)
    indexed, kept, sent = pl.pallas_call(
        outer_rows,
        out_shape=(
            jax.ShapeDtypeStruct((points, pixels), bf16),
            jax.ShapeDtypeStruct((grain_count // 2, pixels), f32),
            jax.ShapeDtypeStruct((grain_count // 2, pixels), bf16),
        ),
        in_specs=[pl.BlockSpec(memory_space=VMEM)] * 10,
        out_specs=[pl.BlockSpec(memory_space=VMEM)] * 3,
        scratch_shapes=[VMEM((32, pixels), f32)],
        compiler_params=params(10),
        name="outer_rows",
    )(point_row, filtered[0], filtered[1], filtered[-2], filtered[-1], low, high, above, below, inner)

    xs, ys = lax.axis_size("x"), lax.axis_size("y")
    trade = []
    for z in range(lax.axis_size("z")):
        for x in range(xs):
            for y in range(ys):
                for core in range(2):
                    at = (z * 2 + core) * xs
                    partner = (((x + core) ^ 1) - core) % xs
                    trade.append(((at + x) * ys + y, (at + partner) * ys + y))
    swapped = lax.ppermute(sent, "core", [(0, 1), (1, 0)])
    chip_sums = (kept + swapped.astype(f32)).astype(bf16)
    parts = lax.all_to_all(chip_sums.reshape(lines, -1, pixels), SCAN, 0, 0, tiled=True)
    group_total = jnp.sum(parts.astype(f32), axis=0).astype(bf16)

    ready, group_total = lax.optimization_barrier((indexed, group_total))
    other = lax.ppermute(ready.reshape(patterns.shape), EVERY, trade)

    block = 512
    own_best = pl.pallas_call(
        own_scores,
        grid=(panels.shape[0] // block,),
        out_shape=jax.ShapeDtypeStruct((1, points), f32),
        in_specs=[
            pl.BlockSpec((points, pixels), lambda i: (0, 0)),
            pl.BlockSpec((block, pixels), lambda i: (i, 0)),
        ],
        out_specs=pl.BlockSpec((1, points), lambda i: (0, 0)),
        scratch_shapes=[VMEM((points, 128), f32)],
        compiler_params=params(20),
        cost_estimate=pl.CostEstimate(
            flops=2 * points * pixels * panels.shape[0],
            bytes_accessed=2 * pixels * panels.shape[0],
            transcendentals=0,
        ),
        name="own_scores",
    )(ready, pltpu.with_memory_space_constraint(panels, pltpu.HBM))
    own_best, group_total, panels = lax.optimization_barrier((own_best, group_total, panels))
    group_totals = lax.all_gather(group_total, DICT, axis=0, tiled=False)
    other, group_totals = lax.optimization_barrier((other, group_totals))
    grain_patterns = pl.pallas_call(
        finish_patterns,
        out_shape=jax.ShapeDtypeStruct((2 * group_total.shape[0], pixels), f32),
        in_specs=[pl.BlockSpec(memory_space=VMEM)],
        out_specs=pl.BlockSpec(memory_space=VMEM),
        compiler_params=params(4),
        name="finish_patterns",
    )(group_totals)
    other_best = pl.pallas_call(
        other_scores,
        out_shape=jax.ShapeDtypeStruct((1, points), f32),
        in_specs=[pl.BlockSpec(memory_space=VMEM)] * 2,
        out_specs=pl.BlockSpec(memory_space=VMEM),
        compiler_params=params(12),
        cost_estimate=pl.CostEstimate(
            flops=2 * points * pixels * panels.shape[0],
            bytes_accessed=2 * pixels * panels.shape[0],
            transcendentals=0,
        ),
        name="other_scores",
    )(other.reshape(points, pixels), panels)
    returned = lax.ppermute(other_best, EVERY, trade)
    max_score = pl.pallas_call(
        functools.partial(finish_scores, pixels=pixels),
        out_shape=jax.ShapeDtypeStruct((tile_rows, tile_cols), f32),
        in_specs=[pl.BlockSpec(memory_space=VMEM)] * 2,
        out_specs=pl.BlockSpec(memory_space=VMEM),
        compiler_params=params(4),
        name="finish_scores",
    )(own_best, returned)
    return (max_score, grain_patterns)


def solution(mesh):
    groups, lines = mesh.shape["dict"], mesh.shape["scan"]
    fine = Mesh(mesh.devices.reshape(groups // 2, 2, lines // 8, 8), EVERY)
    return jax.shard_map(
        shards,
        mesh=fine,
        in_specs=(
            P(SCAN, DICT, None),
            P(),
            P(DICT, None),
            P(SCAN, DICT),
            P(SCAN, DICT),
            P(),
        ),
        out_specs=(P(SCAN, DICT), P(SCAN, None)),
        check_vma=False,
    )
```

```python
import math

import jax
import jax.numpy as jnp
from jax import lax
from jax.experimental import pallas as pl
from jax.experimental.pallas import tpu as pltpu
from jax.sharding import Mesh
from jax.sharding import PartitionSpec as P

SCAN = ("x", "y")
DICT = ("z", "core")
EVERY = ("z", "core", "x", "y")
EPS = 1e-05
VMEM = pltpu.VMEM


def normalise_templates(panel_hbm, out_ref, panel_ref, arrived):
    pixels, lanes = panel_ref.shape
    held = out_ref.shape[0]
    step = pixels // arrived.shape[0]
    copies = []
    for part in range(arrived.shape[0]):
        rows = pl.ds(part * step, step)
        copies.append(pltpu.make_async_copy(panel_hbm.at[rows], panel_ref.at[rows], arrived.at[part]))
        copies[-1].start()
    total = jnp.zeros((1, lanes), jnp.float32)
    for part, copy in enumerate(copies):
        copy.wait()
        values = panel_ref[part * step : (part + 1) * step, :].astype(jnp.float32)
        total = total + jnp.sum(values, axis=0, keepdims=True)
    mean = total * (1.0 / pixels)
    total = jnp.zeros((1, lanes), jnp.float32)
    for start in range(0, pixels, step):
        values = panel_ref[start : start + step, :].astype(jnp.float32) - mean
        total = total + jnp.sum(values * values, axis=0, keepdims=True)
    scale = lax.rsqrt(total * (1.0 / pixels) + EPS)
    first = (lax.axis_index("x") & 1) * held
    lane = lax.broadcasted_iota(jnp.int32, (held, lanes), 1)
    place = lax.broadcasted_iota(jnp.int32, (held, lanes), 0)
    chosen = jnp.where(lane == place + first, 1.0, 0.0).astype(jnp.bfloat16)
    step = 768
    for start in range(0, pixels, step):
        stop = min(start + step, pixels)
        values = (panel_ref[start:stop, :].astype(jnp.float32) - mean) * scale
        out_ref[:, start:stop] = lax.dot_general(
            chosen,
            values.astype(jnp.bfloat16),
            (((1,), (1,)), ((), ())),
            preferred_element_type=jnp.float32,
        ).astype(jnp.bfloat16)


def filter_tile(background_ref, tile_ref, out_ref, low_ref, high_ref, low, high):
    background = background_ref[...].reshape(1, -1)
    rows, _, pixels = tile_ref.shape
    for row in range(rows):
        values = tile_ref[row] - background
        values = values - jnp.sum(values, axis=-1, keepdims=True) * (1.0 / pixels)
        mean_square = jnp.sum(values * values, axis=-1, keepdims=True) * (1.0 / pixels)
        values = (values * lax.rsqrt(mean_square + EPS)).astype(jnp.bfloat16)
        out_ref[row] = values
        low[row : row + 1, :] = values[:1].astype(jnp.float32)
        high[row : row + 1, :] = values[-1:].astype(jnp.float32)
    low_ref[...] = low[...].astype(jnp.bfloat16)
    high_ref[...] = high[...].astype(jnp.bfloat16)


def index_points(column, low, high, shift):
    cols, pixels = column.shape
    shift[7:8, :] = low
    shift[8 : 8 + cols, :] = column
    shift[8 + cols : 9 + cols, :] = high
    total = column + shift[7 : 7 + cols, :] + shift[9 : 9 + cols, :]
    mean_square = jnp.sum(total * total, axis=-1, keepdims=True) * (1.0 / pixels)
    return (total * lax.rsqrt(mean_square + EPS)).astype(jnp.bfloat16)


def inner_rows(tile_ref, low_ref, high_ref, out_ref, low_pad, high_pad, shift, ends):
    rows, cols, pixels = tile_ref.shape
    for side, (pad, side_ref) in enumerate(((low_pad, low_ref), (high_pad, high_ref))):
        pad[...] = side_ref[...].astype(jnp.float32)
        for row in range(1, rows - 1):
            ends[row, side : side + 1, :] = (
                pad[row - 1 : row, :] + pad[row : row + 1, :] + pad[row + 1 : row + 2, :]
            )

    def line(row):
        return tile_ref[row].astype(jnp.float32)

    def one_row(row, carry):
        column = line(row - 1) + line(row) + line(row + 1)
        start = pl.multiple_of((row - 1) * cols, cols)
        out_ref[pl.ds(start, cols), :] = index_points(
            column, ends[row, 0:1, :], ends[row, 1:2, :], shift
        )
        return carry

    lax.fori_loop(1, rows - 1, one_row, 0)


def outer_rows(
    point_row_ref, first_ref, second_ref, third_ref, fourth_ref, low_ref, high_ref, above_ref, below_ref,
    inner_ref, out_ref, kept_ref, sent_ref, shift,
):
    points, pixels = out_ref.shape
    cols = first_ref.shape[0]
    rows = points // cols
    out_ref[cols : points - cols, :] = inner_ref[...]
    low, high = low_ref[...].astype(jnp.float32), high_ref[...].astype(jnp.float32)
    above, below = above_ref[...].astype(jnp.float32), below_ref[...].astype(jnp.float32)
    for halo, near_ref, next_ref, row, inward in (
        (above, first_ref, second_ref, 0, 1),
        (below, fourth_ref, third_ref, rows - 1, -1),
    ):
        column = halo[:cols] + near_ref[...].astype(jnp.float32) + next_ref[...].astype(jnp.float32)
        edges = []
        for side, values in enumerate((low, high)):
            edges.append(
                halo[cols + side : cols + side + 1]
                + values[row : row + 1]
                + values[row + inward : row + inward + 1]
            )
        out_ref[row * cols : (row + 1) * cols, :] = index_points(column, edges[0], edges[1], shift)
    half = kept_ref.shape[0]
    k = lax.broadcasted_iota(jnp.int32, (2 * half, points), 0)
    core = lax.axis_index("core") ^ (k // half)
    grain = (k % half) // 2 * 4 + core * 2 + k % 2
    selector = jnp.where(grain == point_row_ref[...], 1.0, 0.0).astype(jnp.bfloat16)
    step = 1024
    for start in range(0, pixels, step):
        stop = min(start + step, pixels)
        sums = jnp.dot(selector, out_ref[:, start:stop], preferred_element_type=jnp.float32)
        kept_ref[:, start:stop] = sums[:half]
        sent_ref[:, start:stop] = sums[half:].astype(jnp.bfloat16)


def best_scores(own_ref, other_ref, panel_ref, own_best_ref, other_best_ref, points_ref, best_ref):
    points = own_ref.shape[0]
    step = pl.program_id(0)

    @pl.when(step == 0)
    def _():
        points_ref[:points, :] = own_ref[...]
        points_ref[points:, :] = other_ref[...]
        best_ref[...] = jnp.full(best_ref.shape, -jnp.inf, jnp.float32)

    scores = lax.dot_general(
        points_ref[...], panel_ref[...], (((1,), (1,)), ((), ())), preferred_element_type=jnp.float32
    )
    lanes = best_ref.shape[1]
    best = best_ref[...]
    for start in range(0, scores.shape[1], lanes):
        best = jnp.maximum(best, scores[:, start : start + lanes])
    best_ref[...] = best

    @pl.when(step == pl.num_programs(0) - 1)
    def _():
        best = jnp.max(best_ref[...].T, axis=0, keepdims=True)
        own_best_ref[...] = best[:, :points]
        other_best_ref[...] = best[:, points:]


def finish(own_best_ref, returned_ref, totals_ref, max_score_ref, patterns_ref):
    pixels = patterns_ref.shape[1]
    rows, cols = max_score_ref.shape
    best = jnp.maximum(own_best_ref[...], returned_ref[...]) * (1.0 / math.sqrt(pixels))
    for row in range(rows):
        max_score_ref[row : row + 1, :] = best[:, row * cols : (row + 1) * cols]
    groups = totals_ref.shape[0] // 2
    for core in range(2):
        total = totals_ref[core].astype(jnp.float32)
        for group in range(1, groups):
            total = total + totals_ref[2 * group + core].astype(jnp.float32)
        mean_square = jnp.sum(total * total, axis=-1, keepdims=True) * (1.0 / pixels)
        patterns_ref[2 * core : 2 * core + 2, :] = total * lax.rsqrt(mean_square + EPS)


def params(mebibytes):
    return pltpu.CompilerParams(vmem_limit_bytes=mebibytes << 20)


def shards(patterns, background, templates, grain_id, keep_mask, grain_row):
    tile_rows, tile_cols, pixels = patterns.shape
    points = tile_rows * tile_cols
    held = templates.shape[0] // 2
    bf16, f32 = jnp.bfloat16, jnp.float32

    panel = pl.pallas_call(
        normalise_templates,
        out_shape=jax.ShapeDtypeStruct((held, pixels), bf16),
        in_specs=[pl.BlockSpec(memory_space=pl.ANY)],
        out_specs=pl.BlockSpec(memory_space=VMEM),
        scratch_shapes=[VMEM((pixels, 2 * held), bf16), pltpu.SemaphoreType.DMA((5,))],
        compiler_params=params(10),
        name="normalise_templates",
    )(pltpu.with_memory_space_constraint(templates.T, pltpu.HBM))
    panels = lax.all_gather(panel, DICT, axis=0, tiled=True)

    patterns, panel = lax.optimization_barrier((patterns, panel))
    block = tile_rows // 2
    filtered, low_edge, high_edge = pl.pallas_call(
        filter_tile,
        grid=(tile_rows // block,),
        out_shape=(
            jax.ShapeDtypeStruct((tile_rows, tile_cols, pixels), bf16),
            jax.ShapeDtypeStruct((tile_rows, pixels), bf16),
            jax.ShapeDtypeStruct((tile_rows, pixels), bf16),
        ),
        in_specs=[
            pl.BlockSpec((pixels,), lambda i: (0,)),
            pl.BlockSpec((block, tile_cols, pixels), lambda i: (i, 0, 0)),
        ],
        out_specs=(
            pl.BlockSpec((block, tile_cols, pixels), lambda i: (i, 0, 0)),
            pl.BlockSpec((block, pixels), lambda i: (i, 0)),
            pl.BlockSpec((block, pixels), lambda i: (i, 0)),
        ),
        scratch_shapes=[VMEM((block, pixels), f32)] * 2,
        compiler_params=params(16),
        name="filter_tile",
    )(
        pltpu.with_memory_space_constraint(background, pltpu.HBM),
        pltpu.with_memory_space_constraint(patterns, pltpu.HBM),
    )
    columns = lax.axis_size(DICT)
    forward = [(i, i + 1) for i in range(columns - 1)]
    backward = [(i + 1, i) for i in range(columns - 1)]
    low = lax.ppermute(high_edge, DICT, forward)
    high = lax.ppermute(low_edge, DICT, backward)

    def strip(row):
        return jnp.concatenate([filtered[row], low[row : row + 1], high[row : row + 1]], axis=0)

    lines = lax.axis_size(SCAN)
    forward = [(i, i + 1) for i in range(lines - 1)]
    backward = [(i + 1, i) for i in range(lines - 1)]
    above = lax.ppermute(strip(tile_rows - 1), SCAN, forward)
    below = lax.ppermute(strip(0), SCAN, backward)

    grain_count = grain_row.shape[0]
    grain_index = jnp.arange(grain_count, dtype=jnp.int32)
    matches = grain_id.reshape(-1)[:, None] == grain_index[None, :]
    point_row = jnp.sum(jnp.where(matches, grain_row[None, :], 0), axis=1)
    point_row = jnp.where(keep_mask.reshape(-1) == 1, point_row, -1).reshape(1, points)

    inner_points = points - 2 * tile_cols
    inner = pl.pallas_call(
        inner_rows,
        out_shape=jax.ShapeDtypeStruct((inner_points, pixels), bf16),
        in_specs=[pl.BlockSpec(memory_space=VMEM)] * 3,
        out_specs=pl.BlockSpec(memory_space=VMEM),
        scratch_shapes=[VMEM((tile_rows, pixels), f32)] * 2
        + [VMEM((32, pixels), f32), VMEM((tile_rows, 2, pixels), f32)],
        compiler_params=params(10),
        cost_estimate=pl.CostEstimate(
            flops=12 * inner_points * pixels, bytes_accessed=16 * inner_points * pixels, transcendentals=0
        ),
        name="inner_rows",
    )(filtered, low, high)
    indexed, kept, sent = pl.pallas_call(
        outer_rows,
        out_shape=(
            jax.ShapeDtypeStruct((points, pixels), bf16),
            jax.ShapeDtypeStruct((grain_count // 2, pixels), f32),
            jax.ShapeDtypeStruct((grain_count // 2, pixels), bf16),
        ),
        in_specs=[pl.BlockSpec(memory_space=VMEM)] * 10,
        out_specs=[pl.BlockSpec(memory_space=VMEM)] * 3,
        scratch_shapes=[VMEM((32, pixels), f32)],
        compiler_params=params(10),
        name="outer_rows",
    )(point_row, filtered[0], filtered[1], filtered[-2], filtered[-1], low, high, above, below, inner)

    xs, ys = lax.axis_size("x"), lax.axis_size("y")
    trade = []
    for z in range(lax.axis_size("z")):
        for x in range(xs):
            for y in range(ys):
                for core in range(2):
                    at = (z * 2 + core) * xs
                    partner = (((x + core) ^ 1) - core) % xs
                    trade.append(((at + x) * ys + y, (at + partner) * ys + y))
    swapped = lax.ppermute(sent, "core", [(0, 1), (1, 0)])
    other = lax.ppermute(indexed.reshape(patterns.shape), EVERY, trade).reshape(points, pixels)

    chip_sums = (kept + swapped.astype(f32)).astype(bf16)
    chip_sums = chip_sums.reshape(lines, -1, pixels)
    parts = lax.all_to_all(chip_sums, SCAN, 0, 0, tiled=True)
    group_total = jnp.sum(parts.astype(f32), axis=0).astype(bf16)

    block = 512
    copies = jnp.broadcast_to(group_total, (columns,) + group_total.shape)
    group_totals = lax.all_to_all(copies, DICT, 0, 0, tiled=True)
    own_best, other_best = pl.pallas_call(
        best_scores,
        grid=(panels.shape[0] // block,),
        out_shape=(jax.ShapeDtypeStruct((1, points), f32),) * 2,
        in_specs=[
            pl.BlockSpec((points, pixels), lambda i: (0, 0)),
            pl.BlockSpec((points, pixels), lambda i: (0, 0)),
            pl.BlockSpec((block, pixels), lambda i: (i, 0)),
        ],
        out_specs=(pl.BlockSpec((1, points), lambda i: (0, 0)),) * 2,
        scratch_shapes=[VMEM((2 * points, pixels), bf16), VMEM((2 * points, 128), f32)],
        compiler_params=params(28),
        cost_estimate=pl.CostEstimate(
            flops=4 * points * pixels * panels.shape[0],
            bytes_accessed=2 * pixels * panels.shape[0],
            transcendentals=0,
        ),
        name="best_scores",
    )(indexed, other, pltpu.with_memory_space_constraint(panels, pltpu.HBM))
    returned = lax.ppermute(other_best, EVERY, trade)
    returned, group_totals = lax.optimization_barrier((returned, group_totals))
    return pl.pallas_call(
        finish,
        out_shape=(
            jax.ShapeDtypeStruct((tile_rows, tile_cols), f32),
            jax.ShapeDtypeStruct((2 * group_total.shape[0], pixels), f32),
        ),
        in_specs=[pl.BlockSpec(memory_space=VMEM)] * 3,
        out_specs=[pl.BlockSpec(memory_space=VMEM)] * 2,
        compiler_params=params(8),
        name="finish",
    )(own_best, returned, group_totals)


def solution(mesh):
    groups, lines = mesh.shape["dict"], mesh.shape["scan"]
    fine = Mesh(mesh.devices.reshape(groups // 2, 2, lines // 8, 8), EVERY)
    return jax.shard_map(
        shards,
        mesh=fine,
        in_specs=(
            P(SCAN, DICT, None),
            P(),
            P(DICT, None),
            P(SCAN, DICT),
            P(SCAN, DICT),
            P(),
        ),
        out_specs=(P(SCAN, DICT), P(SCAN, None)),
        check_vma=False,
    )
```

```python
import functools
import math

import jax
import jax.numpy as jnp
from jax import lax
from jax.experimental import pallas as pl
from jax.experimental.pallas import tpu as pltpu
from jax.sharding import Mesh
from jax.sharding import PartitionSpec as P

SCAN = ("x", "y")
DICT = ("z", "core")
EVERY = ("z", "core", "x", "y")
EPS = 1e-05
VMEM = pltpu.VMEM


def normalise_templates(panel_hbm, out_ref, panel_ref, arrived):
    pixels, lanes = panel_ref.shape
    held = out_ref.shape[0]
    step = pixels // arrived.shape[0]
    copies = []
    for part in range(arrived.shape[0]):
        rows = pl.ds(part * step, step)
        copies.append(pltpu.make_async_copy(panel_hbm.at[rows], panel_ref.at[rows], arrived.at[part]))
        copies[-1].start()
    total = jnp.zeros((1, lanes), jnp.float32)
    for part, copy in enumerate(copies):
        copy.wait()
        values = panel_ref[part * step : (part + 1) * step, :].astype(jnp.float32)
        total = total + jnp.sum(values, axis=0, keepdims=True)
    mean = total * (1.0 / pixels)
    total = jnp.zeros((1, lanes), jnp.float32)
    for start in range(0, pixels, step):
        values = panel_ref[start : start + step, :].astype(jnp.float32) - mean
        total = total + jnp.sum(values * values, axis=0, keepdims=True)
    scale = lax.rsqrt(total * (1.0 / pixels) + EPS)
    first = (lax.axis_index("x") & 1) * held
    lane = lax.broadcasted_iota(jnp.int32, (held, lanes), 1)
    place = lax.broadcasted_iota(jnp.int32, (held, lanes), 0)
    chosen = jnp.where(lane == place + first, 1.0, 0.0).astype(jnp.bfloat16)
    step = 768
    for start in range(0, pixels, step):
        stop = min(start + step, pixels)
        values = (panel_ref[start:stop, :].astype(jnp.float32) - mean) * scale
        out_ref[:, start:stop] = lax.dot_general(
            chosen,
            values.astype(jnp.bfloat16),
            (((1,), (1,)), ((), ())),
            preferred_element_type=jnp.float32,
        ).astype(jnp.bfloat16)


def filter_tile(background_ref, tile_ref, out_ref, low_ref, high_ref, low, high):
    background = background_ref[...].reshape(1, -1)
    rows, _, pixels = tile_ref.shape
    for row in range(rows):
        values = tile_ref[row] - background
        values = values - jnp.sum(values, axis=-1, keepdims=True) * (1.0 / pixels)
        mean_square = jnp.sum(values * values, axis=-1, keepdims=True) * (1.0 / pixels)
        values = (values * lax.rsqrt(mean_square + EPS)).astype(jnp.bfloat16)
        out_ref[row] = values
        low[row : row + 1, :] = values[:1].astype(jnp.float32)
        high[row : row + 1, :] = values[-1:].astype(jnp.float32)
    low_ref[...] = low[...].astype(jnp.bfloat16)
    high_ref[...] = high[...].astype(jnp.bfloat16)


def index_points(column, low, high, shift):
    cols, pixels = column.shape
    shift[7:8, :] = low
    shift[8 : 8 + cols, :] = column
    shift[8 + cols : 9 + cols, :] = high
    total = column + shift[7 : 7 + cols, :] + shift[9 : 9 + cols, :]
    mean_square = jnp.sum(total * total, axis=-1, keepdims=True) * (1.0 / pixels)
    return (total * lax.rsqrt(mean_square + EPS)).astype(jnp.bfloat16)


def inner_rows(tile_ref, low_ref, high_ref, out_ref, low_pad, high_pad, shift, ends):
    rows, cols, pixels = tile_ref.shape
    for side, (pad, side_ref) in enumerate(((low_pad, low_ref), (high_pad, high_ref))):
        pad[...] = side_ref[...].astype(jnp.float32)
        for row in range(1, rows - 1):
            ends[row, side : side + 1, :] = (
                pad[row - 1 : row, :] + pad[row : row + 1, :] + pad[row + 1 : row + 2, :]
            )

    def line(row):
        return tile_ref[row].astype(jnp.float32)

    def one_row(row, carry):
        column = line(row - 1) + line(row) + line(row + 1)
        start = pl.multiple_of((row - 1) * cols, cols)
        out_ref[pl.ds(start, cols), :] = index_points(
            column, ends[row, 0:1, :], ends[row, 1:2, :], shift
        )
        return carry

    lax.fori_loop(1, rows - 1, one_row, 0)


def outer_rows(
    point_row_ref, first_ref, second_ref, third_ref, fourth_ref, low_ref, high_ref, above_ref, below_ref,
    inner_ref, out_ref, kept_ref, sent_ref, shift,
):
    points, pixels = out_ref.shape
    cols = first_ref.shape[0]
    rows = points // cols
    out_ref[cols : points - cols, :] = inner_ref[...]
    low, high = low_ref[...].astype(jnp.float32), high_ref[...].astype(jnp.float32)
    above, below = above_ref[...].astype(jnp.float32), below_ref[...].astype(jnp.float32)
    for halo, near_ref, next_ref, row, inward in (
        (above, first_ref, second_ref, 0, 1),
        (below, fourth_ref, third_ref, rows - 1, -1),
    ):
        column = halo[:cols] + near_ref[...].astype(jnp.float32) + next_ref[...].astype(jnp.float32)
        edges = []
        for side, values in enumerate((low, high)):
            edges.append(
                halo[cols + side : cols + side + 1]
                + values[row : row + 1]
                + values[row + inward : row + inward + 1]
            )
        out_ref[row * cols : (row + 1) * cols, :] = index_points(column, edges[0], edges[1], shift)
    half = kept_ref.shape[0]
    k = lax.broadcasted_iota(jnp.int32, (2 * half, points), 0)
    core = lax.axis_index("core") ^ (k // half)
    grain = (k % half) // 2 * 4 + core * 2 + k % 2
    selector = jnp.where(grain == point_row_ref[...], 1.0, 0.0).astype(jnp.bfloat16)
    step = 1024
    for start in range(0, pixels, step):
        stop = min(start + step, pixels)
        sums = jnp.dot(selector, out_ref[:, start:stop], preferred_element_type=jnp.float32)
        kept_ref[:, start:stop] = sums[:half]
        sent_ref[:, start:stop] = sums[half:].astype(jnp.bfloat16)


def lane_best(best, scores):
    lanes = best.shape[1]
    for start in range(0, scores.shape[1], lanes):
        best = jnp.maximum(best, scores[:, start : start + lanes])
    return best


def products(points, panel):
    return lax.dot_general(points, panel, (((1,), (1,)), ((), ())), preferred_element_type=jnp.float32)


def best_scores(panel_ref, points_ref, out_ref, best_ref):
    step = pl.program_id(0)

    @pl.when(step == 0)
    def _():
        best_ref[...] = jnp.full(best_ref.shape, -jnp.inf, jnp.float32)

    best = lane_best(best_ref[...], products(points_ref[...], panel_ref[...]))
    best_ref[...] = best

    @pl.when(step == pl.num_programs(0) - 1)
    def _():
        out_ref[...] = jnp.max(best.T, axis=0, keepdims=True)


def finish(own_best_ref, returned_ref, totals_ref, max_score_ref, patterns_ref):
    pixels = patterns_ref.shape[1]
    rows, cols = max_score_ref.shape
    best = jnp.maximum(own_best_ref[...], returned_ref[...]) * (1.0 / math.sqrt(pixels))
    for row in range(rows):
        max_score_ref[row : row + 1, :] = best[:, row * cols : (row + 1) * cols]
    groups = totals_ref.shape[0] // 2
    for core in range(2):
        total = totals_ref[core].astype(jnp.float32)
        for group in range(1, groups):
            total = total + totals_ref[2 * group + core].astype(jnp.float32)
        mean_square = jnp.sum(total * total, axis=-1, keepdims=True) * (1.0 / pixels)
        patterns_ref[2 * core : 2 * core + 2, :] = total * lax.rsqrt(mean_square + EPS)


def params(mebibytes):
    return pltpu.CompilerParams(vmem_limit_bytes=mebibytes << 20)


def shards(patterns, background, templates, grain_id, keep_mask, grain_row):
    tile_rows, tile_cols, pixels = patterns.shape
    points = tile_rows * tile_cols
    held = templates.shape[0] // 2
    bf16, f32 = jnp.bfloat16, jnp.float32

    panel = pl.pallas_call(
        normalise_templates,
        out_shape=jax.ShapeDtypeStruct((held, pixels), bf16),
        in_specs=[pl.BlockSpec(memory_space=pl.ANY)],
        out_specs=pl.BlockSpec(memory_space=VMEM),
        scratch_shapes=[VMEM((pixels, 2 * held), bf16), pltpu.SemaphoreType.DMA((5,))],
        compiler_params=params(10),
        name="normalise_templates",
    )(pltpu.with_memory_space_constraint(templates.T, pltpu.HBM))
    panels = lax.all_gather(panel, DICT, axis=0, tiled=True)

    patterns, panel = lax.optimization_barrier((patterns, panel))
    block = tile_rows // 2
    filtered, low_edge, high_edge = pl.pallas_call(
        filter_tile,
        grid=(tile_rows // block,),
        out_shape=(
            jax.ShapeDtypeStruct((tile_rows, tile_cols, pixels), bf16),
            jax.ShapeDtypeStruct((tile_rows, pixels), bf16),
            jax.ShapeDtypeStruct((tile_rows, pixels), bf16),
        ),
        in_specs=[
            pl.BlockSpec((pixels,), lambda i: (0,)),
            pl.BlockSpec((block, tile_cols, pixels), lambda i: (i, 0, 0)),
        ],
        out_specs=(
            pl.BlockSpec((block, tile_cols, pixels), lambda i: (i, 0, 0)),
            pl.BlockSpec((block, pixels), lambda i: (i, 0)),
            pl.BlockSpec((block, pixels), lambda i: (i, 0)),
        ),
        scratch_shapes=[VMEM((block, pixels), f32)] * 2,
        compiler_params=params(16),
        name="filter_tile",
    )(
        pltpu.with_memory_space_constraint(background, pltpu.HBM),
        pltpu.with_memory_space_constraint(patterns, pltpu.HBM),
    )
    columns = lax.axis_size(DICT)
    forward = [(i, i + 1) for i in range(columns - 1)]
    backward = [(i + 1, i) for i in range(columns - 1)]
    low = lax.ppermute(high_edge, DICT, forward)
    high = lax.ppermute(low_edge, DICT, backward)

    def strip(row):
        return jnp.concatenate([filtered[row], low[row : row + 1], high[row : row + 1]], axis=0)

    lines = lax.axis_size(SCAN)
    forward = [(i, i + 1) for i in range(lines - 1)]
    backward = [(i + 1, i) for i in range(lines - 1)]
    above = lax.ppermute(strip(tile_rows - 1), SCAN, forward)
    below = lax.ppermute(strip(0), SCAN, backward)

    grain_count = grain_row.shape[0]
    grain_index = jnp.arange(grain_count, dtype=jnp.int32)
    matches = grain_id.reshape(-1)[:, None] == grain_index[None, :]
    point_row = jnp.sum(jnp.where(matches, grain_row[None, :], 0), axis=1)
    point_row = jnp.where(keep_mask.reshape(-1) == 1, point_row, -1).reshape(1, points)

    inner_points = points - 2 * tile_cols
    inner = pl.pallas_call(
        inner_rows,
        out_shape=jax.ShapeDtypeStruct((inner_points, pixels), bf16),
        in_specs=[pl.BlockSpec(memory_space=VMEM)] * 3,
        out_specs=pl.BlockSpec(memory_space=VMEM),
        scratch_shapes=[VMEM((tile_rows, pixels), f32)] * 2
        + [VMEM((32, pixels), f32), VMEM((tile_rows, 2, pixels), f32)],
        compiler_params=params(10),
        cost_estimate=pl.CostEstimate(
            flops=12 * inner_points * pixels, bytes_accessed=16 * inner_points * pixels, transcendentals=0
        ),
        name="inner_rows",
    )(filtered, low, high)
    indexed, kept, sent = pl.pallas_call(
        outer_rows,
        out_shape=(
            jax.ShapeDtypeStruct((points, pixels), bf16),
            jax.ShapeDtypeStruct((grain_count // 2, pixels), f32),
            jax.ShapeDtypeStruct((grain_count // 2, pixels), bf16),
        ),
        in_specs=[pl.BlockSpec(memory_space=VMEM)] * 10,
        out_specs=[pl.BlockSpec(memory_space=VMEM)] * 3,
        scratch_shapes=[VMEM((32, pixels), f32)],
        compiler_params=params(10),
        name="outer_rows",
    )(point_row, filtered[0], filtered[1], filtered[-2], filtered[-1], low, high, above, below, inner)

    xs, ys = lax.axis_size("x"), lax.axis_size("y")
    trade = []
    for z in range(lax.axis_size("z")):
        for x in range(xs):
            for y in range(ys):
                for core in range(2):
                    at = (z * 2 + core) * xs
                    partner = (((x + core) ^ 1) - core) % xs
                    trade.append(((at + x) * ys + y, (at + partner) * ys + y))
    swapped = lax.ppermute(sent, "core", [(0, 1), (1, 0)])
    other = lax.ppermute(indexed.reshape(patterns.shape), EVERY, trade).reshape(points, pixels)

    chip_sums = (kept + swapped.astype(f32)).astype(bf16)
    chip_sums = chip_sums.reshape(lines, -1, pixels)
    parts = lax.all_to_all(chip_sums, SCAN, 0, 0, tiled=True)
    block = 512
    scored = functools.partial(
        pl.pallas_call(
            best_scores,
            grid=(panels.shape[0] // block,),
            out_shape=jax.ShapeDtypeStruct((1, points), f32),
            in_specs=[
                pl.BlockSpec((block, pixels), lambda i: (i, 0)),
                pl.BlockSpec((points, pixels), lambda i: (0, 0)),
            ],
            out_specs=pl.BlockSpec((1, points), lambda i: (0, 0)),
            scratch_shapes=[VMEM((points, 128), f32)],
            compiler_params=params(20),
            cost_estimate=pl.CostEstimate(
                flops=2 * points * pixels * panels.shape[0],
                bytes_accessed=2 * pixels * panels.shape[0],
                transcendentals=0,
            ),
            name="best_scores",
        ),
        pltpu.with_memory_space_constraint(panels, pltpu.HBM),
    )
    own_best = scored(indexed)
    own_best, parts = lax.optimization_barrier((own_best, parts))
    group_total = jnp.sum(parts.astype(f32), axis=0).astype(bf16)

    copies = jnp.broadcast_to(group_total, (columns,) + group_total.shape)
    group_totals = lax.all_to_all(copies, DICT, 0, 0, tiled=True)
    other_best = scored(other)
    returned = lax.ppermute(other_best, EVERY, trade)
    returned, group_totals = lax.optimization_barrier((returned, group_totals))
    return pl.pallas_call(
        finish,
        out_shape=(
            jax.ShapeDtypeStruct((tile_rows, tile_cols), f32),
            jax.ShapeDtypeStruct((2 * group_total.shape[0], pixels), f32),
        ),
        in_specs=[pl.BlockSpec(memory_space=VMEM)] * 3,
        out_specs=[pl.BlockSpec(memory_space=VMEM)] * 2,
        compiler_params=params(8),
        name="finish",
    )(own_best, returned, group_totals)


def solution(mesh):
    groups, lines = mesh.shape["dict"], mesh.shape["scan"]
    fine = Mesh(mesh.devices.reshape(groups // 2, 2, lines // 8, 8), EVERY)
    return jax.shard_map(
        shards,
        mesh=fine,
        in_specs=(
            P(SCAN, DICT, None),
            P(),
            P(DICT, None),
            P(SCAN, DICT),
            P(SCAN, DICT),
            P(),
        ),
        out_specs=(P(SCAN, DICT), P(SCAN, None)),
        check_vma=False,
    )
```

```python
import math

import jax
import jax.numpy as jnp
from jax import lax
from jax.experimental import pallas as pl
from jax.experimental.pallas import tpu as pltpu
from jax.sharding import Mesh
from jax.sharding import PartitionSpec as P

SCAN = ("x", "y")
DICT = ("z", "core")
EVERY = ("z", "core", "x", "y")
EPS = 1e-05
VMEM = pltpu.VMEM


def normalise_templates(panel_hbm, out_ref, panel_ref, arrived):
    pixels, lanes = panel_ref.shape
    held = out_ref.shape[0]
    step = pixels // arrived.shape[0]
    copies = []
    for part in range(arrived.shape[0]):
        rows = pl.ds(part * step, step)
        copies.append(pltpu.make_async_copy(panel_hbm.at[rows], panel_ref.at[rows], arrived.at[part]))
        copies[-1].start()
    total = jnp.zeros((1, lanes), jnp.float32)
    for part, copy in enumerate(copies):
        copy.wait()
        values = panel_ref[part * step : (part + 1) * step, :].astype(jnp.float32)
        total = total + jnp.sum(values, axis=0, keepdims=True)
    mean = total * (1.0 / pixels)
    total = jnp.zeros((1, lanes), jnp.float32)
    for start in range(0, pixels, step):
        values = panel_ref[start : start + step, :].astype(jnp.float32) - mean
        total = total + jnp.sum(values * values, axis=0, keepdims=True)
    scale = lax.rsqrt(total * (1.0 / pixels) + EPS)
    first = (lax.axis_index("x") & 1) * held
    lane = lax.broadcasted_iota(jnp.int32, (held, lanes), 1)
    place = lax.broadcasted_iota(jnp.int32, (held, lanes), 0)
    chosen = jnp.where(lane == place + first, 1.0, 0.0).astype(jnp.bfloat16)
    step = 768
    for start in range(0, pixels, step):
        stop = min(start + step, pixels)
        values = (panel_ref[start:stop, :].astype(jnp.float32) - mean) * scale
        out_ref[:, start:stop] = lax.dot_general(
            chosen,
            values.astype(jnp.bfloat16),
            (((1,), (1,)), ((), ())),
            preferred_element_type=jnp.float32,
        ).astype(jnp.bfloat16)


def filter_tile(background_ref, tile_ref, out_ref, low_ref, high_ref, low, high):
    background = background_ref[...].reshape(1, -1)
    rows, _, pixels = tile_ref.shape
    for row in range(rows):
        values = tile_ref[row] - background
        values = values - jnp.sum(values, axis=-1, keepdims=True) * (1.0 / pixels)
        mean_square = jnp.sum(values * values, axis=-1, keepdims=True) * (1.0 / pixels)
        values = (values * lax.rsqrt(mean_square + EPS)).astype(jnp.bfloat16)
        out_ref[row] = values
        low[row : row + 1, :] = values[:1].astype(jnp.float32)
        high[row : row + 1, :] = values[-1:].astype(jnp.float32)
    low_ref[...] = low[...].astype(jnp.bfloat16)
    high_ref[...] = high[...].astype(jnp.bfloat16)


def index_points(column, low, high, shift):
    cols, pixels = column.shape
    shift[7:8, :] = low
    shift[8 : 8 + cols, :] = column
    shift[8 + cols : 9 + cols, :] = high
    total = column + shift[7 : 7 + cols, :] + shift[9 : 9 + cols, :]
    mean_square = jnp.sum(total * total, axis=-1, keepdims=True) * (1.0 / pixels)
    return (total * lax.rsqrt(mean_square + EPS)).astype(jnp.bfloat16)


def inner_rows(tile_ref, low_ref, high_ref, out_ref, low_pad, high_pad, shift, ends):
    rows, cols, pixels = tile_ref.shape
    for side, (pad, side_ref) in enumerate(((low_pad, low_ref), (high_pad, high_ref))):
        pad[...] = side_ref[...].astype(jnp.float32)
        for row in range(1, rows - 1):
            ends[row, side : side + 1, :] = (
                pad[row - 1 : row, :] + pad[row : row + 1, :] + pad[row + 1 : row + 2, :]
            )

    def line(row):
        return tile_ref[row].astype(jnp.float32)

    def one_row(row, carry):
        column = line(row - 1) + line(row) + line(row + 1)
        start = pl.multiple_of((row - 1) * cols, cols)
        out_ref[pl.ds(start, cols), :] = index_points(
            column, ends[row, 0:1, :], ends[row, 1:2, :], shift
        )
        return carry

    lax.fori_loop(1, rows - 1, one_row, 0)


def outer_rows(
    point_row_ref, first_ref, second_ref, third_ref, fourth_ref, low_ref, high_ref, above_ref, below_ref,
    inner_ref, out_ref, kept_ref, sent_ref, shift,
):
    points, pixels = out_ref.shape
    cols = first_ref.shape[0]
    rows = points // cols
    out_ref[cols : points - cols, :] = inner_ref[...]
    low, high = low_ref[...].astype(jnp.float32), high_ref[...].astype(jnp.float32)
    above, below = above_ref[...].astype(jnp.float32), below_ref[...].astype(jnp.float32)
    for halo, near_ref, next_ref, row, inward in (
        (above, first_ref, second_ref, 0, 1),
        (below, fourth_ref, third_ref, rows - 1, -1),
    ):
        column = halo[:cols] + near_ref[...].astype(jnp.float32) + next_ref[...].astype(jnp.float32)
        edges = []
        for side, values in enumerate((low, high)):
            edges.append(
                halo[cols + side : cols + side + 1]
                + values[row : row + 1]
                + values[row + inward : row + inward + 1]
            )
        out_ref[row * cols : (row + 1) * cols, :] = index_points(column, edges[0], edges[1], shift)
    half = kept_ref.shape[0]
    k = lax.broadcasted_iota(jnp.int32, (2 * half, points), 0)
    core = lax.axis_index("core") ^ (k // half)
    grain = (k % half) // 2 * 4 + core * 2 + k % 2
    selector = jnp.where(grain == point_row_ref[...], 1.0, 0.0).astype(jnp.bfloat16)
    step = 1024
    for start in range(0, pixels, step):
        stop = min(start + step, pixels)
        sums = jnp.dot(selector, out_ref[:, start:stop], preferred_element_type=jnp.float32)
        kept_ref[:, start:stop] = sums[:half]
        sent_ref[:, start:stop] = sums[half:].astype(jnp.bfloat16)


def best_scores(own_ref, other_ref, panel_ref, own_best_ref, other_best_ref, points_ref, best_ref):
    points = own_ref.shape[0]
    step = pl.program_id(0)

    @pl.when(step == 0)
    def _():
        points_ref[:points, :] = own_ref[...]
        points_ref[points:, :] = other_ref[...]
        best_ref[...] = jnp.full(best_ref.shape, -jnp.inf, jnp.float32)

    scores = lax.dot_general(
        points_ref[...], panel_ref[...], (((1,), (1,)), ((), ())), preferred_element_type=jnp.float32
    )
    lanes = best_ref.shape[1]
    best = best_ref[...]
    for start in range(0, scores.shape[1], lanes):
        best = jnp.maximum(best, scores[:, start : start + lanes])
    best_ref[...] = best

    @pl.when(step == pl.num_programs(0) - 1)
    def _():
        best = jnp.max(best_ref[...].T, axis=0, keepdims=True)
        own_best_ref[...] = best[:, :points]
        other_best_ref[...] = best[:, points:]


def finish(own_best_ref, returned_ref, totals_ref, max_score_ref, patterns_ref):
    pixels = patterns_ref.shape[1]
    rows, cols = max_score_ref.shape
    best = jnp.maximum(own_best_ref[...], returned_ref[...]) * (1.0 / math.sqrt(pixels))
    for row in range(rows):
        max_score_ref[row : row + 1, :] = best[:, row * cols : (row + 1) * cols]
    groups = totals_ref.shape[0] // 2
    for core in range(2):
        total = totals_ref[core].astype(jnp.float32)
        for group in range(1, groups):
            total = total + totals_ref[2 * group + core].astype(jnp.float32)
        mean_square = jnp.sum(total * total, axis=-1, keepdims=True) * (1.0 / pixels)
        patterns_ref[2 * core : 2 * core + 2, :] = total * lax.rsqrt(mean_square + EPS)


def params(mebibytes):
    return pltpu.CompilerParams(vmem_limit_bytes=mebibytes << 20)


def shards(patterns, background, templates, grain_id, keep_mask, grain_row):
    tile_rows, tile_cols, pixels = patterns.shape
    points = tile_rows * tile_cols
    held = templates.shape[0] // 2
    bf16, f32 = jnp.bfloat16, jnp.float32

    panel = pl.pallas_call(
        normalise_templates,
        out_shape=jax.ShapeDtypeStruct((held, pixels), bf16),
        in_specs=[pl.BlockSpec(memory_space=pl.ANY)],
        out_specs=pl.BlockSpec(memory_space=VMEM),
        scratch_shapes=[VMEM((pixels, 2 * held), bf16), pltpu.SemaphoreType.DMA((5,))],
        compiler_params=params(10),
        name="normalise_templates",
    )(pltpu.with_memory_space_constraint(templates.T, pltpu.HBM))
    panels = lax.all_gather(panel, DICT, axis=0, tiled=True)

    patterns, panel = lax.optimization_barrier((patterns, panel))
    block = tile_rows // 2
    filtered, low_edge, high_edge = pl.pallas_call(
        filter_tile,
        grid=(tile_rows // block,),
        out_shape=(
            jax.ShapeDtypeStruct((tile_rows, tile_cols, pixels), bf16),
            jax.ShapeDtypeStruct((tile_rows, pixels), bf16),
            jax.ShapeDtypeStruct((tile_rows, pixels), bf16),
        ),
        in_specs=[
            pl.BlockSpec((pixels,), lambda i: (0,)),
            pl.BlockSpec((block, tile_cols, pixels), lambda i: (i, 0, 0)),
        ],
        out_specs=(
            pl.BlockSpec((block, tile_cols, pixels), lambda i: (i, 0, 0)),
            pl.BlockSpec((block, pixels), lambda i: (i, 0)),
            pl.BlockSpec((block, pixels), lambda i: (i, 0)),
        ),
        scratch_shapes=[VMEM((block, pixels), f32)] * 2,
        compiler_params=params(16),
        name="filter_tile",
    )(
        pltpu.with_memory_space_constraint(background, pltpu.HBM),
        pltpu.with_memory_space_constraint(patterns, pltpu.HBM),
    )
    columns = lax.axis_size(DICT)
    forward = [(i, i + 1) for i in range(columns - 1)]
    backward = [(i + 1, i) for i in range(columns - 1)]
    low = lax.ppermute(high_edge, DICT, forward)
    high = lax.ppermute(low_edge, DICT, backward)

    def strip(row):
        return jnp.concatenate([filtered[row], low[row : row + 1], high[row : row + 1]], axis=0)

    lines = lax.axis_size(SCAN)
    forward = [(i, i + 1) for i in range(lines - 1)]
    backward = [(i + 1, i) for i in range(lines - 1)]
    above = lax.ppermute(strip(tile_rows - 1), SCAN, forward)
    below = lax.ppermute(strip(0), SCAN, backward)

    grain_count = grain_row.shape[0]
    grain_index = jnp.arange(grain_count, dtype=jnp.int32)
    matches = grain_id.reshape(-1)[:, None] == grain_index[None, :]
    point_row = jnp.sum(jnp.where(matches, grain_row[None, :], 0), axis=1)
    point_row = jnp.where(keep_mask.reshape(-1) == 1, point_row, -1).reshape(1, points)

    inner_points = points - 2 * tile_cols
    inner = pl.pallas_call(
        inner_rows,
        out_shape=jax.ShapeDtypeStruct((inner_points, pixels), bf16),
        in_specs=[pl.BlockSpec(memory_space=VMEM)] * 3,
        out_specs=pl.BlockSpec(memory_space=VMEM),
        scratch_shapes=[VMEM((tile_rows, pixels), f32)] * 2
        + [VMEM((32, pixels), f32), VMEM((tile_rows, 2, pixels), f32)],
        compiler_params=params(10),
        cost_estimate=pl.CostEstimate(
            flops=12 * inner_points * pixels, bytes_accessed=16 * inner_points * pixels, transcendentals=0
        ),
        name="inner_rows",
    )(filtered, low, high)
    indexed, kept, sent = pl.pallas_call(
        outer_rows,
        out_shape=(
            jax.ShapeDtypeStruct((points, pixels), bf16),
            jax.ShapeDtypeStruct((grain_count // 2, pixels), f32),
            jax.ShapeDtypeStruct((grain_count // 2, pixels), bf16),
        ),
        in_specs=[pl.BlockSpec(memory_space=VMEM)] * 10,
        out_specs=[pl.BlockSpec(memory_space=VMEM)] * 3,
        scratch_shapes=[VMEM((32, pixels), f32)],
        compiler_params=params(10),
        name="outer_rows",
    )(point_row, filtered[0], filtered[1], filtered[-2], filtered[-1], low, high, above, below, inner)

    xs, ys = lax.axis_size("x"), lax.axis_size("y")
    trade = []
    for z in range(lax.axis_size("z")):
        for x in range(xs):
            for y in range(ys):
                for core in range(2):
                    at = (z * 2 + core) * xs
                    partner = (((x + core) ^ 1) - core) % xs
                    trade.append(((at + x) * ys + y, (at + partner) * ys + y))
    swapped = lax.ppermute(sent, "core", [(0, 1), (1, 0)])
    other = lax.ppermute(indexed.reshape(patterns.shape), EVERY, trade).reshape(points, pixels)

    chip_sums = (kept + swapped.astype(f32)).astype(bf16)
    chip_sums = chip_sums.reshape(lines, -1, pixels)
    parts = lax.all_to_all(chip_sums, SCAN, 0, 0, tiled=True)
    block = 512
    own_best, other_best = pl.pallas_call(
        best_scores,
        grid=(panels.shape[0] // block,),
        out_shape=(jax.ShapeDtypeStruct((1, points), f32),) * 2,
        in_specs=[
            pl.BlockSpec((points, pixels), lambda i: (0, 0)),
            pl.BlockSpec((points, pixels), lambda i: (0, 0)),
            pl.BlockSpec((block, pixels), lambda i: (i, 0)),
        ],
        out_specs=(pl.BlockSpec((1, points), lambda i: (0, 0)),) * 2,
        scratch_shapes=[VMEM((2 * points, pixels), bf16), VMEM((2 * points, 128), f32)],
        compiler_params=params(28),
        cost_estimate=pl.CostEstimate(
            flops=4 * points * pixels * panels.shape[0],
            bytes_accessed=2 * pixels * panels.shape[0],
            transcendentals=0,
        ),
        name="best_scores",
    )(
        pltpu.with_memory_space_constraint(indexed, pltpu.HBM),
        pltpu.with_memory_space_constraint(other, pltpu.HBM),
        pltpu.with_memory_space_constraint(panels, pltpu.HBM),
    )
    returned = lax.ppermute(other_best, EVERY, trade)
    other_best, parts = lax.optimization_barrier((other_best, parts))
    group_total = jnp.sum(parts.astype(f32), axis=0).astype(bf16)
    group_totals = lax.all_gather(group_total, DICT, axis=0, tiled=False)
    returned, group_totals = lax.optimization_barrier((returned, group_totals))
    return pl.pallas_call(
        finish,
        out_shape=(
            jax.ShapeDtypeStruct((tile_rows, tile_cols), f32),
            jax.ShapeDtypeStruct((2 * group_total.shape[0], pixels), f32),
        ),
        in_specs=[pl.BlockSpec(memory_space=VMEM)] * 3,
        out_specs=[pl.BlockSpec(memory_space=VMEM)] * 2,
        compiler_params=params(8),
        name="finish",
    )(own_best, returned, group_totals)


def solution(mesh):
    groups, lines = mesh.shape["dict"], mesh.shape["scan"]
    fine = Mesh(mesh.devices.reshape(groups // 2, 2, lines // 8, 8), EVERY)
    return jax.shard_map(
        shards,
        mesh=fine,
        in_specs=(
            P(SCAN, DICT, None),
            P(),
            P(DICT, None),
            P(SCAN, DICT),
            P(SCAN, DICT),
            P(),
        ),
        out_specs=(P(SCAN, DICT), P(SCAN, None)),
        check_vma=False,
    )
```

```python
import functools
import math

import jax
import jax.numpy as jnp
from jax import lax
from jax.experimental import pallas as pl
from jax.experimental.pallas import tpu as pltpu
from jax.sharding import Mesh
from jax.sharding import PartitionSpec as P

SCAN = ("x", "y")
DICT = ("z", "core")
EVERY = ("z", "core", "x", "y")
EPS = 1e-05
VMEM = pltpu.VMEM


def normalise_templates(panel_hbm, out_ref, panel_ref, arrived):
    pixels, lanes = panel_ref.shape
    held = out_ref.shape[0]
    step = pixels // arrived.shape[0]
    copies = []
    for part in range(arrived.shape[0]):
        rows = pl.ds(part * step, step)
        copies.append(pltpu.make_async_copy(panel_hbm.at[rows], panel_ref.at[rows], arrived.at[part]))
        copies[-1].start()
    total = jnp.zeros((1, lanes), jnp.float32)
    for part, copy in enumerate(copies):
        copy.wait()
        values = panel_ref[part * step : (part + 1) * step, :].astype(jnp.float32)
        total = total + jnp.sum(values, axis=0, keepdims=True)
    mean = total * (1.0 / pixels)
    total = jnp.zeros((1, lanes), jnp.float32)
    for start in range(0, pixels, step):
        values = panel_ref[start : start + step, :].astype(jnp.float32) - mean
        total = total + jnp.sum(values * values, axis=0, keepdims=True)
    scale = lax.rsqrt(total * (1.0 / pixels) + EPS)
    first = ((lax.axis_index("x") + lax.axis_index("y")) & 1) * held
    lane = lax.broadcasted_iota(jnp.int32, (held, lanes), 1)
    place = lax.broadcasted_iota(jnp.int32, (held, lanes), 0)
    chosen = jnp.where(lane == place + first, 1.0, 0.0).astype(jnp.bfloat16)
    step = 768
    for start in range(0, pixels, step):
        stop = min(start + step, pixels)
        values = (panel_ref[start:stop, :].astype(jnp.float32) - mean) * scale
        out_ref[:, start:stop] = lax.dot_general(
            chosen,
            values.astype(jnp.bfloat16),
            (((1,), (1,)), ((), ())),
            preferred_element_type=jnp.float32,
        ).astype(jnp.bfloat16)


def filter_tile(background_ref, tile_ref, out_ref, low_ref, high_ref, low, high):
    background = background_ref[...].reshape(1, -1)
    rows, _, pixels = tile_ref.shape
    for row in range(rows):
        values = tile_ref[row] - background
        values = values - jnp.sum(values, axis=-1, keepdims=True) * (1.0 / pixels)
        mean_square = jnp.sum(values * values, axis=-1, keepdims=True) * (1.0 / pixels)
        values = (values * lax.rsqrt(mean_square + EPS)).astype(jnp.bfloat16)
        out_ref[row] = values
        low[row : row + 1, :] = values[:1].astype(jnp.float32)
        high[row : row + 1, :] = values[-1:].astype(jnp.float32)
    low_ref[...] = low[...].astype(jnp.bfloat16)
    high_ref[...] = high[...].astype(jnp.bfloat16)


def index_points(column, low, high, shift):
    cols, pixels = column.shape
    shift[7:8, :] = low
    shift[8 : 8 + cols, :] = column
    shift[8 + cols : 9 + cols, :] = high
    total = column + shift[7 : 7 + cols, :] + shift[9 : 9 + cols, :]
    mean_square = jnp.sum(total * total, axis=-1, keepdims=True) * (1.0 / pixels)
    return (total * lax.rsqrt(mean_square + EPS)).astype(jnp.bfloat16)


def inner_rows(tile_ref, low_ref, high_ref, out_ref, low_pad, high_pad, shift, ends):
    rows, cols, pixels = tile_ref.shape
    for side, (pad, side_ref) in enumerate(((low_pad, low_ref), (high_pad, high_ref))):
        pad[...] = side_ref[...].astype(jnp.float32)
        for row in range(1, rows - 1):
            ends[row, side : side + 1, :] = (
                pad[row - 1 : row, :] + pad[row : row + 1, :] + pad[row + 1 : row + 2, :]
            )

    def line(row):
        return tile_ref[row].astype(jnp.float32)

    def one_row(row, carry):
        column = line(row - 1) + line(row) + line(row + 1)
        start = pl.multiple_of((row - 1) * cols, cols)
        out_ref[pl.ds(start, cols), :] = index_points(
            column, ends[row, 0:1, :], ends[row, 1:2, :], shift
        )
        return carry

    lax.fori_loop(1, rows - 1, one_row, 0)


def outer_rows(
    point_row_ref, first_ref, second_ref, third_ref, fourth_ref, low_ref, high_ref, above_ref, below_ref,
    inner_ref, upper_ref, lower_ref, kept_ref, sent_ref, shift,
):
    middle, pixels = upper_ref.shape
    cols = first_ref.shape[0]
    points = 2 * middle
    last = points // cols - 1
    upper_ref[cols:, :] = inner_ref[: middle - cols, :]
    lower_ref[: middle - cols, :] = inner_ref[middle - cols :, :]
    low, high = low_ref[...].astype(jnp.float32), high_ref[...].astype(jnp.float32)
    above, below = above_ref[...].astype(jnp.float32), below_ref[...].astype(jnp.float32)
    for out_ref, start, halo, near_ref, next_ref, row, inward in (
        (upper_ref, 0, above, first_ref, second_ref, 0, 1),
        (lower_ref, middle - cols, below, fourth_ref, third_ref, last, -1),
    ):
        column = halo[:cols] + near_ref[...].astype(jnp.float32) + next_ref[...].astype(jnp.float32)
        edges = []
        for side, values in enumerate((low, high)):
            edges.append(
                halo[cols + side : cols + side + 1]
                + values[row : row + 1]
                + values[row + inward : row + inward + 1]
            )
        out_ref[start : start + cols, :] = index_points(column, edges[0], edges[1], shift)
    half = kept_ref.shape[0]
    k = lax.broadcasted_iota(jnp.int32, (2 * half, points), 0)
    core = lax.axis_index("core") ^ (k // half)
    grain = (k % half) // 2 * 4 + core * 2 + k % 2
    selector = jnp.where(grain == point_row_ref[...], 1.0, 0.0).astype(jnp.bfloat16)
    step = 1024
    for start in range(0, pixels, step):
        stop = min(start + step, pixels)
        sums = jnp.dot(
            selector[:, :middle], upper_ref[:, start:stop], preferred_element_type=jnp.float32
        ) + jnp.dot(selector[:, middle:], lower_ref[:, start:stop], preferred_element_type=jnp.float32)
        kept_ref[:, start:stop] = sums[:half]
        sent_ref[:, start:stop] = sums[half:].astype(jnp.bfloat16)


def lane_best(best, scores):
    lanes = best.shape[1]
    for start in range(0, scores.shape[1], lanes):
        best = jnp.maximum(best, scores[:, start : start + lanes])
    return best


def products(points, panel):
    return lax.dot_general(points, panel, (((1,), (1,)), ((), ())), preferred_element_type=jnp.float32)


def best_scores(panel_ref, first_ref, second_ref, out_ref, points_ref, best_ref):
    step = pl.program_id(0)

    @pl.when(step == 0)
    def _():
        half = first_ref.shape[0]
        points_ref[:half, :] = first_ref[...]
        points_ref[half:, :] = second_ref[...]
        best_ref[...] = jnp.full(best_ref.shape, -jnp.inf, jnp.float32)

    best = lane_best(best_ref[...], products(points_ref[...], panel_ref[...]))
    best_ref[...] = best

    @pl.when(step == pl.num_programs(0) - 1)
    def _():
        out_ref[...] = jnp.max(best.T, axis=0, keepdims=True)


def finish(own_best_ref, returned_ref, totals_ref, max_score_ref, patterns_ref):
    pixels = patterns_ref.shape[1]
    rows, cols = max_score_ref.shape
    best = jnp.maximum(own_best_ref[...], returned_ref[...]) * (1.0 / math.sqrt(pixels))
    for row in range(rows):
        max_score_ref[row : row + 1, :] = best[:, row * cols : (row + 1) * cols]
    groups = totals_ref.shape[0] // 2
    for core in range(2):
        total = totals_ref[core].astype(jnp.float32)
        for group in range(1, groups):
            total = total + totals_ref[2 * group + core].astype(jnp.float32)
        mean_square = jnp.sum(total * total, axis=-1, keepdims=True) * (1.0 / pixels)
        patterns_ref[2 * core : 2 * core + 2, :] = total * lax.rsqrt(mean_square + EPS)


def params(mebibytes):
    return pltpu.CompilerParams(vmem_limit_bytes=mebibytes << 20)


def shards(patterns, background, templates, grain_id, keep_mask, grain_row):
    tile_rows, tile_cols, pixels = patterns.shape
    points = tile_rows * tile_cols
    held = templates.shape[0] // 2
    bf16, f32 = jnp.bfloat16, jnp.float32

    panel = pl.pallas_call(
        normalise_templates,
        out_shape=jax.ShapeDtypeStruct((held, pixels), bf16),
        in_specs=[pl.BlockSpec(memory_space=pl.ANY)],
        out_specs=pl.BlockSpec(memory_space=VMEM),
        scratch_shapes=[VMEM((pixels, 2 * held), bf16), pltpu.SemaphoreType.DMA((5,))],
        compiler_params=params(10),
        name="normalise_templates",
    )(pltpu.with_memory_space_constraint(templates.T, pltpu.HBM))
    panels = lax.all_gather(panel, DICT, axis=0, tiled=True)

    patterns, panel = lax.optimization_barrier((patterns, panel))
    block = tile_rows // 2
    filtered, low_edge, high_edge = pl.pallas_call(
        filter_tile,
        grid=(tile_rows // block,),
        out_shape=(
            jax.ShapeDtypeStruct((tile_rows, tile_cols, pixels), bf16),
            jax.ShapeDtypeStruct((tile_rows, pixels), bf16),
            jax.ShapeDtypeStruct((tile_rows, pixels), bf16),
        ),
        in_specs=[
            pl.BlockSpec((pixels,), lambda i: (0,)),
            pl.BlockSpec((block, tile_cols, pixels), lambda i: (i, 0, 0)),
        ],
        out_specs=(
            pl.BlockSpec((block, tile_cols, pixels), lambda i: (i, 0, 0)),
            pl.BlockSpec((block, pixels), lambda i: (i, 0)),
            pl.BlockSpec((block, pixels), lambda i: (i, 0)),
        ),
        scratch_shapes=[VMEM((block, pixels), f32)] * 2,
        compiler_params=params(16),
        name="filter_tile",
    )(
        pltpu.with_memory_space_constraint(background, pltpu.HBM),
        pltpu.with_memory_space_constraint(patterns, pltpu.HBM),
    )
    columns = lax.axis_size(DICT)
    forward = [(i, i + 1) for i in range(columns - 1)]
    backward = [(i + 1, i) for i in range(columns - 1)]
    low = lax.ppermute(high_edge, DICT, forward)
    high = lax.ppermute(low_edge, DICT, backward)

    def strip(row):
        return jnp.concatenate([filtered[row], low[row : row + 1], high[row : row + 1]], axis=0)

    lines = lax.axis_size(SCAN)
    forward = [(i, i + 1) for i in range(lines - 1)]
    backward = [(i + 1, i) for i in range(lines - 1)]
    above = lax.ppermute(strip(tile_rows - 1), SCAN, forward)
    below = lax.ppermute(strip(0), SCAN, backward)

    grain_count = grain_row.shape[0]
    grain_index = jnp.arange(grain_count, dtype=jnp.int32)
    matches = grain_id.reshape(-1)[:, None] == grain_index[None, :]
    point_row = jnp.sum(jnp.where(matches, grain_row[None, :], 0), axis=1)
    point_row = jnp.where(keep_mask.reshape(-1) == 1, point_row, -1).reshape(1, points)

    inner_points = points - 2 * tile_cols
    inner = pl.pallas_call(
        inner_rows,
        out_shape=jax.ShapeDtypeStruct((inner_points, pixels), bf16),
        in_specs=[pl.BlockSpec(memory_space=VMEM)] * 3,
        out_specs=pl.BlockSpec(memory_space=VMEM),
        scratch_shapes=[VMEM((tile_rows, pixels), f32)] * 2
        + [VMEM((32, pixels), f32), VMEM((tile_rows, 2, pixels), f32)],
        compiler_params=params(10),
        cost_estimate=pl.CostEstimate(
            flops=12 * inner_points * pixels, bytes_accessed=16 * inner_points * pixels, transcendentals=0
        ),
        name="inner_rows",
    )(filtered, low, high)
    upper, lower, kept, sent = pl.pallas_call(
        outer_rows,
        out_shape=(
            jax.ShapeDtypeStruct((points // 2, pixels), bf16),
            jax.ShapeDtypeStruct((points // 2, pixels), bf16),
            jax.ShapeDtypeStruct((grain_count // 2, pixels), f32),
            jax.ShapeDtypeStruct((grain_count // 2, pixels), bf16),
        ),
        in_specs=[pl.BlockSpec(memory_space=VMEM)] * 10,
        out_specs=[pl.BlockSpec(memory_space=VMEM)] * 4,
        scratch_shapes=[VMEM((32, pixels), f32)],
        compiler_params=params(10),
        name="outer_rows",
    )(point_row, filtered[0], filtered[1], filtered[-2], filtered[-1], low, high, above, below, inner)

    xs, ys = lax.axis_size("x"), lax.axis_size("y")
    trades = ([], [])
    for z in range(lax.axis_size("z")):
        for core in range(2):
            for x in range(xs):
                for y in range(ys):
                    at = (z * 2 + core) * xs
                    beside = (((x + core) ^ 1) - core) % xs
                    trades[0].append(((at + x) * ys + y, (at + beside) * ys + y))
                    beside = (((y + core) ^ 1) - core) % ys
                    trades[1].append(((at + x) * ys + y, (at + x) * ys + beside))
    swapped = lax.ppermute(sent, "core", [(0, 1), (1, 0)])
    others = [
        lax.ppermute(half.reshape(-1, tile_cols, pixels), EVERY, trade).reshape(half.shape)
        for half, trade in zip((upper, lower), trades)
    ]

    chip_sums = (kept + swapped.astype(f32)).astype(bf16)
    chip_sums = chip_sums.reshape(lines, -1, pixels)
    parts = lax.all_to_all(chip_sums, SCAN, 0, 0, tiled=True)
    block = 512
    scored = functools.partial(
        pl.pallas_call(
            best_scores,
            grid=(panels.shape[0] // block,),
            out_shape=jax.ShapeDtypeStruct((1, points), f32),
            in_specs=[
                pl.BlockSpec((block, pixels), lambda i: (i, 0)),
                pl.BlockSpec((points // 2, pixels), lambda i: (0, 0)),
                pl.BlockSpec((points // 2, pixels), lambda i: (0, 0)),
            ],
            out_specs=pl.BlockSpec((1, points), lambda i: (0, 0)),
            scratch_shapes=[VMEM((points, pixels), bf16), VMEM((points, 128), f32)],
            compiler_params=params(20),
            cost_estimate=pl.CostEstimate(
                flops=2 * points * pixels * panels.shape[0],
                bytes_accessed=2 * pixels * panels.shape[0],
                transcendentals=0,
            ),
            name="best_scores",
        ),
        pltpu.with_memory_space_constraint(panels, pltpu.HBM),
    )
    own_best = scored(upper, lower)
    own_best, parts = lax.optimization_barrier((own_best, parts))
    group_total = jnp.sum(parts.astype(f32), axis=0).astype(bf16)

    copies = jnp.broadcast_to(group_total, (columns,) + group_total.shape)
    group_totals = lax.all_to_all(copies, DICT, 0, 0, tiled=True)
    other_best = scored(*others)
    returned = [
        lax.ppermute(best, EVERY, trade) for best, trade in zip(jnp.split(other_best, 2, axis=1), trades)
    ]
    returned = jnp.concatenate(returned, axis=1)
    returned, group_totals = lax.optimization_barrier((returned, group_totals))
    return pl.pallas_call(
        finish,
        out_shape=(
            jax.ShapeDtypeStruct((tile_rows, tile_cols), f32),
            jax.ShapeDtypeStruct((2 * group_total.shape[0], pixels), f32),
        ),
        in_specs=[pl.BlockSpec(memory_space=VMEM)] * 3,
        out_specs=[pl.BlockSpec(memory_space=VMEM)] * 2,
        compiler_params=params(8),
        name="finish",
    )(own_best, returned, group_totals)


def solution(mesh):
    groups, lines = mesh.shape["dict"], mesh.shape["scan"]
    fine = Mesh(mesh.devices.reshape(groups // 2, 2, lines // 8, 8), EVERY)
    return jax.shard_map(
        shards,
        mesh=fine,
        in_specs=(
            P(SCAN, DICT, None),
            P(),
            P(DICT, None),
            P(SCAN, DICT),
            P(SCAN, DICT),
            P(),
        ),
        out_specs=(P(SCAN, DICT), P(SCAN, None)),
        check_vma=False,
    )
```

```python
import functools
import math

import jax
import jax.numpy as jnp
from jax import lax
from jax.experimental import pallas as pl
from jax.experimental.pallas import tpu as pltpu
from jax.sharding import Mesh
from jax.sharding import PartitionSpec as P

SCAN = ("x", "y")
DICT = ("z", "core")
EVERY = ("z", "core", "x", "y")
EPS = 1e-05
VMEM = pltpu.VMEM


def normalise_templates(panel_hbm, out_ref, panel_ref, arrived):
    pixels, lanes = panel_ref.shape
    held = out_ref.shape[0]
    step = pixels // arrived.shape[0]
    copies = []
    for part in range(arrived.shape[0]):
        rows = pl.ds(part * step, step)
        copies.append(pltpu.make_async_copy(panel_hbm.at[rows], panel_ref.at[rows], arrived.at[part]))
        copies[-1].start()
    total = jnp.zeros((1, lanes), jnp.float32)
    for part, copy in enumerate(copies):
        copy.wait()
        values = panel_ref[part * step : (part + 1) * step, :].astype(jnp.float32)
        total = total + jnp.sum(values, axis=0, keepdims=True)
    mean = total * (1.0 / pixels)
    total = jnp.zeros((1, lanes), jnp.float32)
    for start in range(0, pixels, step):
        values = panel_ref[start : start + step, :].astype(jnp.float32) - mean
        total = total + jnp.sum(values * values, axis=0, keepdims=True)
    scale = lax.rsqrt(total * (1.0 / pixels) + EPS)
    first = (lax.axis_index("x") & 1) * held
    lane = lax.broadcasted_iota(jnp.int32, (held, lanes), 1)
    place = lax.broadcasted_iota(jnp.int32, (held, lanes), 0)
    chosen = jnp.where(lane == place + first, 1.0, 0.0).astype(jnp.bfloat16)
    step = 768
    for start in range(0, pixels, step):
        stop = min(start + step, pixels)
        values = (panel_ref[start:stop, :].astype(jnp.float32) - mean) * scale
        out_ref[:, start:stop] = lax.dot_general(
            chosen,
            values.astype(jnp.bfloat16),
            (((1,), (1,)), ((), ())),
            preferred_element_type=jnp.float32,
        ).astype(jnp.bfloat16)


def filter_tile(background_ref, tile_ref, out_ref, low_ref, high_ref, low, high):
    background = background_ref[...].reshape(1, -1)
    rows, _, pixels = tile_ref.shape
    for row in range(rows):
        values = tile_ref[row] - background
        values = values - jnp.sum(values, axis=-1, keepdims=True) * (1.0 / pixels)
        mean_square = jnp.sum(values * values, axis=-1, keepdims=True) * (1.0 / pixels)
        values = (values * lax.rsqrt(mean_square + EPS)).astype(jnp.bfloat16)
        out_ref[row] = values
        low[row : row + 1, :] = values[:1].astype(jnp.float32)
        high[row : row + 1, :] = values[-1:].astype(jnp.float32)
    low_ref[...] = low[...].astype(jnp.bfloat16)
    high_ref[...] = high[...].astype(jnp.bfloat16)


def index_points(column, low, high, shift):
    cols, pixels = column.shape
    shift[7:8, :] = low
    shift[8 : 8 + cols, :] = column
    shift[8 + cols : 9 + cols, :] = high
    total = column + shift[7 : 7 + cols, :] + shift[9 : 9 + cols, :]
    mean_square = jnp.sum(total * total, axis=-1, keepdims=True) * (1.0 / pixels)
    return (total * lax.rsqrt(mean_square + EPS)).astype(jnp.bfloat16)


def inner_rows(tile_ref, low_ref, high_ref, out_ref, low_pad, high_pad, shift, ends):
    rows, cols, pixels = tile_ref.shape
    for side, (pad, side_ref) in enumerate(((low_pad, low_ref), (high_pad, high_ref))):
        pad[...] = side_ref[...].astype(jnp.float32)
        for row in range(1, rows - 1):
            ends[row, side : side + 1, :] = (
                pad[row - 1 : row, :] + pad[row : row + 1, :] + pad[row + 1 : row + 2, :]
            )

    def line(row):
        return tile_ref[row].astype(jnp.float32)

    def one_row(row, carry):
        column = line(row - 1) + line(row) + line(row + 1)
        start = pl.multiple_of((row - 1) * cols, cols)
        out_ref[pl.ds(start, cols), :] = index_points(
            column, ends[row, 0:1, :], ends[row, 1:2, :], shift
        )
        return carry

    lax.fori_loop(1, rows - 1, one_row, 0)


def outer_rows(
    point_row_ref, first_ref, second_ref, third_ref, fourth_ref, low_ref, high_ref, above_ref, below_ref,
    inner_ref, out_ref, kept_ref, sent_ref, shift,
):
    points, pixels = out_ref.shape
    cols = first_ref.shape[0]
    rows = points // cols
    out_ref[cols : points - cols, :] = inner_ref[...]
    low, high = low_ref[...].astype(jnp.float32), high_ref[...].astype(jnp.float32)
    above, below = above_ref[...].astype(jnp.float32), below_ref[...].astype(jnp.float32)
    for halo, near_ref, next_ref, row, inward in (
        (above, first_ref, second_ref, 0, 1),
        (below, fourth_ref, third_ref, rows - 1, -1),
    ):
        column = halo[:cols] + near_ref[...].astype(jnp.float32) + next_ref[...].astype(jnp.float32)
        edges = []
        for side, values in enumerate((low, high)):
            edges.append(
                halo[cols + side : cols + side + 1]
                + values[row : row + 1]
                + values[row + inward : row + inward + 1]
            )
        out_ref[row * cols : (row + 1) * cols, :] = index_points(column, edges[0], edges[1], shift)
    half = kept_ref.shape[0]
    k = lax.broadcasted_iota(jnp.int32, (2 * half, points), 0)
    core = lax.axis_index("core") ^ (k // half)
    grain = (k % half) // 2 * 4 + core * 2 + k % 2
    selector = jnp.where(grain == point_row_ref[...], 1.0, 0.0).astype(jnp.bfloat16)
    step = 1024
    for start in range(0, pixels, step):
        stop = min(start + step, pixels)
        sums = jnp.dot(selector, out_ref[:, start:stop], preferred_element_type=jnp.float32)
        kept_ref[:, start:stop] = sums[:half]
        sent_ref[:, start:stop] = sums[half:].astype(jnp.bfloat16)


def lane_best(best, scores):
    lanes = best.shape[1]
    for start in range(0, scores.shape[1], lanes):
        best = jnp.maximum(best, scores[:, start : start + lanes])
    return best


def products(points, panel):
    return lax.dot_general(points, panel, (((1,), (1,)), ((), ())), preferred_element_type=jnp.float32)


def best_scores(panel_ref, points_ref, out_ref, best_ref):
    step = pl.program_id(0)

    @pl.when(step == 0)
    def _():
        best_ref[...] = jnp.full(best_ref.shape, -jnp.inf, jnp.float32)

    best = lane_best(best_ref[...], products(points_ref[...], panel_ref[...]))
    best_ref[...] = best

    @pl.when(step == pl.num_programs(0) - 1)
    def _():
        out_ref[...] = jnp.max(best.T, axis=0, keepdims=True)


def finish(own_best_ref, returned_ref, totals_ref, max_score_ref, patterns_ref):
    pixels = patterns_ref.shape[1]
    rows, cols = max_score_ref.shape
    best = jnp.maximum(own_best_ref[...], returned_ref[...]) * (1.0 / math.sqrt(pixels))
    for row in range(rows):
        max_score_ref[row : row + 1, :] = best[:, row * cols : (row + 1) * cols]
    groups = totals_ref.shape[0] // 2
    for core in range(2):
        total = totals_ref[core].astype(jnp.float32)
        for group in range(1, groups):
            total = total + totals_ref[2 * group + core].astype(jnp.float32)
        mean_square = jnp.sum(total * total, axis=-1, keepdims=True) * (1.0 / pixels)
        patterns_ref[2 * core : 2 * core + 2, :] = total * lax.rsqrt(mean_square + EPS)


def params(mebibytes):
    return pltpu.CompilerParams(vmem_limit_bytes=mebibytes << 20)


def shards(patterns, background, templates, grain_id, keep_mask, grain_row):
    tile_rows, tile_cols, pixels = patterns.shape
    points = tile_rows * tile_cols
    held = templates.shape[0] // 2
    bf16, f32 = jnp.bfloat16, jnp.float32

    panel = pl.pallas_call(
        normalise_templates,
        out_shape=jax.ShapeDtypeStruct((held, pixels), bf16),
        in_specs=[pl.BlockSpec(memory_space=pl.ANY)],
        out_specs=pl.BlockSpec(memory_space=VMEM),
        scratch_shapes=[VMEM((pixels, 2 * held), bf16), pltpu.SemaphoreType.DMA((5,))],
        compiler_params=params(10),
        name="normalise_templates",
    )(pltpu.with_memory_space_constraint(templates.T, pltpu.HBM))
    panels = lax.all_gather(panel, DICT, axis=0, tiled=True)

    patterns, panel = lax.optimization_barrier((patterns, panel))
    block = tile_rows // 2
    filtered, low_edge, high_edge = pl.pallas_call(
        filter_tile,
        grid=(tile_rows // block,),
        out_shape=(
            jax.ShapeDtypeStruct((tile_rows, tile_cols, pixels), bf16),
            jax.ShapeDtypeStruct((tile_rows, pixels), bf16),
            jax.ShapeDtypeStruct((tile_rows, pixels), bf16),
        ),
        in_specs=[
            pl.BlockSpec((pixels,), lambda i: (0,)),
            pl.BlockSpec((block, tile_cols, pixels), lambda i: (i, 0, 0)),
        ],
        out_specs=(
            pl.BlockSpec((block, tile_cols, pixels), lambda i: (i, 0, 0)),
            pl.BlockSpec((block, pixels), lambda i: (i, 0)),
            pl.BlockSpec((block, pixels), lambda i: (i, 0)),
        ),
        scratch_shapes=[VMEM((block, pixels), f32)] * 2,
        compiler_params=params(16),
        name="filter_tile",
    )(
        pltpu.with_memory_space_constraint(background, pltpu.HBM),
        pltpu.with_memory_space_constraint(patterns, pltpu.HBM),
    )
    columns = lax.axis_size(DICT)
    forward = [(i, i + 1) for i in range(columns - 1)]
    backward = [(i + 1, i) for i in range(columns - 1)]
    low = lax.ppermute(high_edge, DICT, forward)
    high = lax.ppermute(low_edge, DICT, backward)

    def strip(row):
        return jnp.concatenate([filtered[row], low[row : row + 1], high[row : row + 1]], axis=0)

    lines = lax.axis_size(SCAN)
    forward = [(i, i + 1) for i in range(lines - 1)]
    backward = [(i + 1, i) for i in range(lines - 1)]
    above = lax.ppermute(strip(tile_rows - 1), SCAN, forward)
    first = strip(0)
    first, _ = lax.optimization_barrier((first, strip(tile_rows - 1)))
    below = lax.ppermute(first, SCAN, backward)

    grain_count = grain_row.shape[0]
    grain_index = jnp.arange(grain_count, dtype=jnp.int32)
    matches = grain_id.reshape(-1)[:, None] == grain_index[None, :]
    point_row = jnp.sum(jnp.where(matches, grain_row[None, :], 0), axis=1)
    point_row = jnp.where(keep_mask.reshape(-1) == 1, point_row, -1).reshape(1, points)

    inner_points = points - 2 * tile_cols
    inner = pl.pallas_call(
        inner_rows,
        out_shape=jax.ShapeDtypeStruct((inner_points, pixels), bf16),
        in_specs=[pl.BlockSpec(memory_space=VMEM)] * 3,
        out_specs=pl.BlockSpec(memory_space=VMEM),
        scratch_shapes=[VMEM((tile_rows, pixels), f32)] * 2
        + [VMEM((32, pixels), f32), VMEM((tile_rows, 2, pixels), f32)],
        compiler_params=params(10),
        cost_estimate=pl.CostEstimate(
            flops=12 * inner_points * pixels, bytes_accessed=16 * inner_points * pixels, transcendentals=0
        ),
        name="inner_rows",
    )(filtered, low, high)
    indexed, kept, sent = pl.pallas_call(
        outer_rows,
        out_shape=(
            jax.ShapeDtypeStruct((points, pixels), bf16),
            jax.ShapeDtypeStruct((grain_count // 2, pixels), f32),
            jax.ShapeDtypeStruct((grain_count // 2, pixels), bf16),
        ),
        in_specs=[pl.BlockSpec(memory_space=VMEM)] * 10,
        out_specs=[pl.BlockSpec(memory_space=VMEM)] * 3,
        scratch_shapes=[VMEM((32, pixels), f32)],
        compiler_params=params(10),
        name="outer_rows",
    )(point_row, filtered[0], filtered[1], filtered[-2], filtered[-1], low, high, above, below, inner)

    xs, ys = lax.axis_size("x"), lax.axis_size("y")
    trade = []
    for z in range(lax.axis_size("z")):
        for x in range(xs):
            for y in range(ys):
                for core in range(2):
                    at = (z * 2 + core) * xs
                    partner = (((x + core) ^ 1) - core) % xs
                    trade.append(((at + x) * ys + y, (at + partner) * ys + y))
    swapped = lax.ppermute(sent, "core", [(0, 1), (1, 0)])
    other = lax.ppermute(indexed.reshape(patterns.shape), EVERY, trade).reshape(points, pixels)

    chip_sums = (kept + swapped.astype(f32)).astype(bf16)
    chip_sums = chip_sums.reshape(lines, -1, pixels)
    parts = lax.all_to_all(chip_sums, SCAN, 0, 0, tiled=True)
    block = 512
    scored = functools.partial(
        pl.pallas_call(
            best_scores,
            grid=(panels.shape[0] // block,),
            out_shape=jax.ShapeDtypeStruct((1, points), f32),
            in_specs=[
                pl.BlockSpec((block, pixels), lambda i: (i, 0)),
                pl.BlockSpec((points, pixels), lambda i: (0, 0)),
            ],
            out_specs=pl.BlockSpec((1, points), lambda i: (0, 0)),
            scratch_shapes=[VMEM((points, 128), f32)],
            compiler_params=params(20),
            cost_estimate=pl.CostEstimate(
                flops=2 * points * pixels * panels.shape[0],
                bytes_accessed=2 * pixels * panels.shape[0],
                transcendentals=0,
            ),
            name="best_scores",
        ),
        pltpu.with_memory_space_constraint(panels, pltpu.HBM),
    )
    own_best = scored(indexed)
    own_best, parts = lax.optimization_barrier((own_best, parts))
    group_total = jnp.sum(parts.astype(f32), axis=0).astype(bf16)

    copies = jnp.broadcast_to(group_total, (columns,) + group_total.shape)
    group_totals = lax.all_to_all(copies, DICT, 0, 0, tiled=True)
    other_best = scored(other)
    returned = lax.ppermute(other_best, EVERY, trade)
    returned, group_totals = lax.optimization_barrier((returned, group_totals))
    return pl.pallas_call(
        finish,
        out_shape=(
            jax.ShapeDtypeStruct((tile_rows, tile_cols), f32),
            jax.ShapeDtypeStruct((2 * group_total.shape[0], pixels), f32),
        ),
        in_specs=[pl.BlockSpec(memory_space=VMEM)] * 3,
        out_specs=[pl.BlockSpec(memory_space=VMEM)] * 2,
        compiler_params=params(8),
        name="finish",
    )(own_best, returned, group_totals)


def solution(mesh):
    groups, lines = mesh.shape["dict"], mesh.shape["scan"]
    fine = Mesh(mesh.devices.reshape(groups // 2, 2, lines // 8, 8), EVERY)
    return jax.shard_map(
        shards,
        mesh=fine,
        in_specs=(
            P(SCAN, DICT, None),
            P(),
            P(DICT, None),
            P(SCAN, DICT),
            P(SCAN, DICT),
            P(),
        ),
        out_specs=(P(SCAN, DICT), P(SCAN, None)),
        check_vma=False,
    )
```

```python
import functools
import math

import jax
import jax.numpy as jnp
from jax import lax
from jax.experimental import pallas as pl
from jax.experimental.pallas import tpu as pltpu
from jax.sharding import Mesh
from jax.sharding import PartitionSpec as P

SCAN = ("x", "y")
DICT = ("z", "core")
EVERY = ("z", "core", "x", "y")
EPS = 1e-05
VMEM = pltpu.VMEM


def normalise_templates(panel_hbm, out_ref, panel_ref, arrived):
    pixels, lanes = panel_ref.shape
    held = out_ref.shape[0]
    step = pixels // arrived.shape[0]
    copies = []
    for part in range(arrived.shape[0]):
        rows = pl.ds(part * step, step)
        copies.append(pltpu.make_async_copy(panel_hbm.at[rows], panel_ref.at[rows], arrived.at[part]))
        copies[-1].start()
    total = jnp.zeros((1, lanes), jnp.float32)
    for part, copy in enumerate(copies):
        copy.wait()
        values = panel_ref[part * step : (part + 1) * step, :].astype(jnp.float32)
        total = total + jnp.sum(values, axis=0, keepdims=True)
    mean = total * (1.0 / pixels)
    total = jnp.zeros((1, lanes), jnp.float32)
    for start in range(0, pixels, step):
        values = panel_ref[start : start + step, :].astype(jnp.float32) - mean
        total = total + jnp.sum(values * values, axis=0, keepdims=True)
    scale = lax.rsqrt(total * (1.0 / pixels) + EPS)
    first = (lax.axis_index("x") & 1) * held
    lane = lax.broadcasted_iota(jnp.int32, (held, lanes), 1)
    place = lax.broadcasted_iota(jnp.int32, (held, lanes), 0)
    chosen = jnp.where(lane == place + first, 1.0, 0.0).astype(jnp.bfloat16)
    step = 768
    for start in range(0, pixels, step):
        stop = min(start + step, pixels)
        values = (panel_ref[start:stop, :].astype(jnp.float32) - mean) * scale
        out_ref[:, start:stop] = lax.dot_general(
            chosen,
            values.astype(jnp.bfloat16),
            (((1,), (1,)), ((), ())),
            preferred_element_type=jnp.float32,
        ).astype(jnp.bfloat16)


def filter_tile(background_ref, tile_ref, out_ref, low_ref, high_ref, low, high):
    background = background_ref[...].reshape(1, -1)
    rows, _, pixels = tile_ref.shape
    for row in range(rows):
        values = tile_ref[row] - background
        values = values - jnp.sum(values, axis=-1, keepdims=True) * (1.0 / pixels)
        mean_square = jnp.sum(values * values, axis=-1, keepdims=True) * (1.0 / pixels)
        values = (values * lax.rsqrt(mean_square + EPS)).astype(jnp.bfloat16)
        out_ref[row] = values
        low[row : row + 1, :] = values[:1].astype(jnp.float32)
        high[row : row + 1, :] = values[-1:].astype(jnp.float32)
    low_ref[...] = low[...].astype(jnp.bfloat16)
    high_ref[...] = high[...].astype(jnp.bfloat16)


def index_points(column, low, high, shift):
    cols, pixels = column.shape
    shift[7:8, :] = low
    shift[8 : 8 + cols, :] = column
    shift[8 + cols : 9 + cols, :] = high
    total = column + shift[7 : 7 + cols, :] + shift[9 : 9 + cols, :]
    mean_square = jnp.sum(total * total, axis=-1, keepdims=True) * (1.0 / pixels)
    return (total * lax.rsqrt(mean_square + EPS)).astype(jnp.bfloat16)


def inner_rows(tile_ref, low_ref, high_ref, out_ref, low_pad, high_pad, shift, ends):
    rows, cols, pixels = tile_ref.shape
    for side, (pad, side_ref) in enumerate(((low_pad, low_ref), (high_pad, high_ref))):
        pad[...] = side_ref[...].astype(jnp.float32)
        for row in range(1, rows - 1):
            ends[row, side : side + 1, :] = (
                pad[row - 1 : row, :] + pad[row : row + 1, :] + pad[row + 1 : row + 2, :]
            )

    def line(row):
        return tile_ref[row].astype(jnp.float32)

    def one_row(row, carry):
        column = line(row - 1) + line(row) + line(row + 1)
        start = pl.multiple_of((row - 1) * cols, cols)
        out_ref[pl.ds(start, cols), :] = index_points(
            column, ends[row, 0:1, :], ends[row, 1:2, :], shift
        )
        return carry

    lax.fori_loop(1, rows - 1, one_row, 0)


def outer_rows(
    point_row_ref, first_ref, second_ref, third_ref, fourth_ref, low_ref, high_ref, above_ref, below_ref,
    inner_ref, out_ref, kept_ref, sent_ref, shift,
):
    points, pixels = out_ref.shape
    cols = first_ref.shape[0]
    rows = points // cols
    out_ref[cols : points - cols, :] = inner_ref[...]
    low, high = low_ref[...].astype(jnp.float32), high_ref[...].astype(jnp.float32)
    above, below = above_ref[...].astype(jnp.float32), below_ref[...].astype(jnp.float32)
    for halo, near_ref, next_ref, row, inward in (
        (above, first_ref, second_ref, 0, 1),
        (below, fourth_ref, third_ref, rows - 1, -1),
    ):
        column = halo[:cols] + near_ref[...].astype(jnp.float32) + next_ref[...].astype(jnp.float32)
        edges = []
        for side, values in enumerate((low, high)):
            edges.append(
                halo[cols + side : cols + side + 1]
                + values[row : row + 1]
                + values[row + inward : row + inward + 1]
            )
        out_ref[row * cols : (row + 1) * cols, :] = index_points(column, edges[0], edges[1], shift)
    half = kept_ref.shape[0]
    k = lax.broadcasted_iota(jnp.int32, (2 * half, points), 0)
    core = lax.axis_index("core") ^ (k // half)
    grain = (k % half) // 2 * 4 + core * 2 + k % 2
    selector = jnp.where(grain == point_row_ref[...], 1.0, 0.0).astype(jnp.bfloat16)
    step = 1024
    for start in range(0, pixels, step):
        stop = min(start + step, pixels)
        sums = jnp.dot(selector, out_ref[:, start:stop], preferred_element_type=jnp.float32)
        kept_ref[:, start:stop] = sums[:half]
        sent_ref[:, start:stop] = sums[half:].astype(jnp.bfloat16)


def lane_best(best, scores):
    lanes = best.shape[1]
    for start in range(0, scores.shape[1], lanes):
        best = jnp.maximum(best, scores[:, start : start + lanes])
    return best


def products(points, panel):
    return lax.dot_general(points, panel, (((1,), (1,)), ((), ())), preferred_element_type=jnp.float32)


def best_scores(panel_ref, points_ref, out_ref, best_ref):
    step = pl.program_id(0)

    @pl.when(step == 0)
    def _():
        best_ref[...] = jnp.full(best_ref.shape, -jnp.inf, jnp.float32)

    best = lane_best(best_ref[...], products(points_ref[...], panel_ref[...]))
    best_ref[...] = best

    @pl.when(step == pl.num_programs(0) - 1)
    def _():
        out_ref[...] = jnp.max(best.T, axis=0, keepdims=True)


def sum_and_repeat(parts_ref, out_ref):
    total = jnp.sum(parts_ref[...].astype(jnp.float32), axis=0).astype(jnp.bfloat16)
    for copy in range(out_ref.shape[0]):
        out_ref[copy] = total


def finish(own_best_ref, returned_ref, totals_ref, max_score_ref, patterns_ref):
    pixels = patterns_ref.shape[1]
    rows, cols = max_score_ref.shape
    best = jnp.maximum(own_best_ref[...], returned_ref[...]) * (1.0 / math.sqrt(pixels))
    for row in range(rows):
        max_score_ref[row : row + 1, :] = best[:, row * cols : (row + 1) * cols]
    groups = totals_ref.shape[0] // 2
    for core in range(2):
        total = totals_ref[core].astype(jnp.float32)
        for group in range(1, groups):
            total = total + totals_ref[2 * group + core].astype(jnp.float32)
        mean_square = jnp.sum(total * total, axis=-1, keepdims=True) * (1.0 / pixels)
        patterns_ref[2 * core : 2 * core + 2, :] = total * lax.rsqrt(mean_square + EPS)


def params(mebibytes):
    return pltpu.CompilerParams(vmem_limit_bytes=mebibytes << 20)


def shards(patterns, background, templates, grain_id, keep_mask, grain_row):
    tile_rows, tile_cols, pixels = patterns.shape
    points = tile_rows * tile_cols
    held = templates.shape[0] // 2
    bf16, f32 = jnp.bfloat16, jnp.float32

    panel = pl.pallas_call(
        normalise_templates,
        out_shape=jax.ShapeDtypeStruct((held, pixels), bf16),
        in_specs=[pl.BlockSpec(memory_space=pl.ANY)],
        out_specs=pl.BlockSpec(memory_space=VMEM),
        scratch_shapes=[VMEM((pixels, 2 * held), bf16), pltpu.SemaphoreType.DMA((5,))],
        compiler_params=params(10),
        name="normalise_templates",
    )(pltpu.with_memory_space_constraint(templates.T, pltpu.HBM))
    panels = lax.all_gather(panel, DICT, axis=0, tiled=True)

    patterns, panel = lax.optimization_barrier((patterns, panel))
    block = tile_rows // 2
    filtered, low_edge, high_edge = pl.pallas_call(
        filter_tile,
        grid=(tile_rows // block,),
        out_shape=(
            jax.ShapeDtypeStruct((tile_rows, tile_cols, pixels), bf16),
            jax.ShapeDtypeStruct((tile_rows, pixels), bf16),
            jax.ShapeDtypeStruct((tile_rows, pixels), bf16),
        ),
        in_specs=[
            pl.BlockSpec((pixels,), lambda i: (0,)),
            pl.BlockSpec((block, tile_cols, pixels), lambda i: (i, 0, 0)),
        ],
        out_specs=(
            pl.BlockSpec((block, tile_cols, pixels), lambda i: (i, 0, 0)),
            pl.BlockSpec((block, pixels), lambda i: (i, 0)),
            pl.BlockSpec((block, pixels), lambda i: (i, 0)),
        ),
        scratch_shapes=[VMEM((block, pixels), f32)] * 2,
        compiler_params=params(16),
        name="filter_tile",
    )(
        pltpu.with_memory_space_constraint(background, pltpu.HBM),
        pltpu.with_memory_space_constraint(patterns, pltpu.HBM),
    )
    columns = lax.axis_size(DICT)
    forward = [(i, i + 1) for i in range(columns - 1)]
    backward = [(i + 1, i) for i in range(columns - 1)]
    low = lax.ppermute(high_edge, DICT, forward)
    high = lax.ppermute(low_edge, DICT, backward)

    def strip(row):
        return jnp.concatenate([filtered[row], low[row : row + 1], high[row : row + 1]], axis=0)

    lines = lax.axis_size(SCAN)
    forward = [(i, i + 1) for i in range(lines - 1)]
    backward = [(i + 1, i) for i in range(lines - 1)]
    above = lax.ppermute(strip(tile_rows - 1), SCAN, forward)
    first = strip(0)
    first, _ = lax.optimization_barrier((first, strip(tile_rows - 1)))
    below = lax.ppermute(first, SCAN, backward)

    grain_count = grain_row.shape[0]
    grain_index = jnp.arange(grain_count, dtype=jnp.int32)
    matches = grain_id.reshape(-1)[:, None] == grain_index[None, :]
    point_row = jnp.sum(jnp.where(matches, grain_row[None, :], 0), axis=1)
    point_row = jnp.where(keep_mask.reshape(-1) == 1, point_row, -1).reshape(1, points)

    inner_points = points - 2 * tile_cols
    inner = pl.pallas_call(
        inner_rows,
        out_shape=jax.ShapeDtypeStruct((inner_points, pixels), bf16),
        in_specs=[pl.BlockSpec(memory_space=VMEM)] * 3,
        out_specs=pl.BlockSpec(memory_space=VMEM),
        scratch_shapes=[VMEM((tile_rows, pixels), f32)] * 2
        + [VMEM((32, pixels), f32), VMEM((tile_rows, 2, pixels), f32)],
        compiler_params=params(10),
        cost_estimate=pl.CostEstimate(
            flops=12 * inner_points * pixels, bytes_accessed=16 * inner_points * pixels, transcendentals=0
        ),
        name="inner_rows",
    )(filtered, low, high)
    indexed, kept, sent = pl.pallas_call(
        outer_rows,
        out_shape=(
            jax.ShapeDtypeStruct((points, pixels), bf16),
            jax.ShapeDtypeStruct((grain_count // 2, pixels), f32),
            jax.ShapeDtypeStruct((grain_count // 2, pixels), bf16),
        ),
        in_specs=[pl.BlockSpec(memory_space=VMEM)] * 10,
        out_specs=[pl.BlockSpec(memory_space=VMEM)] * 3,
        scratch_shapes=[VMEM((32, pixels), f32)],
        compiler_params=params(10),
        name="outer_rows",
    )(point_row, filtered[0], filtered[1], filtered[-2], filtered[-1], low, high, above, below, inner)

    xs, ys = lax.axis_size("x"), lax.axis_size("y")
    trade = []
    for z in range(lax.axis_size("z")):
        for x in range(xs):
            for y in range(ys):
                for core in range(2):
                    at = (z * 2 + core) * xs
                    partner = (((x + core) ^ 1) - core) % xs
                    trade.append(((at + x) * ys + y, (at + partner) * ys + y))
    swapped = lax.ppermute(sent, "core", [(0, 1), (1, 0)])
    other = lax.ppermute(indexed.reshape(patterns.shape), EVERY, trade).reshape(points, pixels)

    chip_sums = (kept + swapped.astype(f32)).astype(bf16)
    chip_sums = chip_sums.reshape(lines, -1, pixels)
    parts = lax.all_to_all(chip_sums, SCAN, 0, 0, tiled=True)
    block = 512
    scored = functools.partial(
        pl.pallas_call(
            best_scores,
            grid=(panels.shape[0] // block,),
            out_shape=jax.ShapeDtypeStruct((1, points), f32),
            in_specs=[
                pl.BlockSpec((block, pixels), lambda i: (i, 0)),
                pl.BlockSpec((points, pixels), lambda i: (0, 0)),
            ],
            out_specs=pl.BlockSpec((1, points), lambda i: (0, 0)),
            scratch_shapes=[VMEM((points, 128), f32)],
            compiler_params=params(20),
            cost_estimate=pl.CostEstimate(
                flops=2 * points * pixels * panels.shape[0],
                bytes_accessed=2 * pixels * panels.shape[0],
                transcendentals=0,
            ),
            name="best_scores",
        ),
        pltpu.with_memory_space_constraint(panels, pltpu.HBM),
    )
    own_best = scored(indexed)
    own_best, parts = lax.optimization_barrier((own_best, parts))
    copies = pl.pallas_call(
        sum_and_repeat,
        out_shape=jax.ShapeDtypeStruct((columns,) + parts.shape[1:], bf16),
        in_specs=[pl.BlockSpec(memory_space=VMEM)],
        out_specs=pl.BlockSpec(memory_space=VMEM),
        compiler_params=params(4),
        name="sum_and_repeat",
    )(parts)
    group_totals = lax.all_to_all(copies, DICT, 0, 0, tiled=True)
    other_best = scored(other)
    returned = lax.ppermute(other_best, EVERY, trade)
    returned, group_totals = lax.optimization_barrier((returned, group_totals))
    return pl.pallas_call(
        finish,
        out_shape=(
            jax.ShapeDtypeStruct((tile_rows, tile_cols), f32),
            jax.ShapeDtypeStruct((2 * parts.shape[1], pixels), f32),
        ),
        in_specs=[pl.BlockSpec(memory_space=VMEM)] * 3,
        out_specs=[pl.BlockSpec(memory_space=VMEM)] * 2,
        compiler_params=params(8),
        name="finish",
    )(own_best, returned, group_totals)


def solution(mesh):
    groups, lines = mesh.shape["dict"], mesh.shape["scan"]
    fine = Mesh(mesh.devices.reshape(groups // 2, 2, lines // 8, 8), EVERY)
    return jax.shard_map(
        shards,
        mesh=fine,
        in_specs=(
            P(SCAN, DICT, None),
            P(),
            P(DICT, None),
            P(SCAN, DICT),
            P(SCAN, DICT),
            P(),
        ),
        out_specs=(P(SCAN, DICT), P(SCAN, None)),
        check_vma=False,
    )
```
